32 devices in a mesh: vec: 8 (over z, y), space: 4 (over x, core).
Axes of the slice: x: 2, y: 2, z: 4, core: 2. Of those that a mesh axis runs over, the one named last changes fastest.
Arguments:
- perturbation: float32 [8, 6, 96, 512], P('vec', None, 'space'), may hold values from -40 to 40
- trajectory: bfloat16 [8, 3, 6, 96, 512], P('vec', None, None, 'space'), may hold values from -1.796875 to 1.796875
- step_order: int32 [8], replicated, may hold values from 0 to 7, each once
Outputs:
- ortho_vectors: float32 [8, 6, 96, 512], P('vec', None, 'space')
- upper_factor: float32 [8, 8], replicated
The draws below stay inside these ranges and needn't reach their ends.
Inputs may be any that keep to these rules, and one draw needn't show every extreme that they name: `step_order`: each number appears once.
All inputs are finite; a program needn't handle non-finite values.
Results may differ from the reference program's by a relative error of at most 0.0003.
Values may be sent and summed in bfloat16 or wider, within the bound.
A program may use at most 64 MiB of HBM per device.

```python
import jax
import jax.numpy as jnp
from jax import lax

NY = 512
STEPS = 2
K = 8
NX = 96
TRAJ = 8


def draw_perturbation(key, part):
    noise = jnp.clip(jax.random.normal(jax.random.fold_in(key, 11), (K, 6, NX, NY), jnp.float32), -6.0, 6.0)
    return noise


def levels(own_key, shape, split, low, top_value):
    factor_of = 1.0
    for position, blocks in split:
        heights = jax.random.uniform(jax.random.fold_in(jax.random.fold_in(own_key, 6), position), (blocks,), jnp.float32, low / len(split), top_value / len(split))
        factor_of = factor_of * jnp.repeat(jnp.exp(heights), shape[position] // blocks).reshape((-1,) + (1,) * (len(shape) - 1 - position))
    return factor_of


def gaussian(stream_key, extent, width, bound, cuts=(), dtype=jnp.bfloat16):
    array = width * jax.random.normal(stream_key, extent, jnp.float32)
    if cuts:
        array = array * levels(stream_key, extent, cuts, -0.22, 0.18)
    return jnp.clip(array, -bound, bound).astype(dtype)


def setup_inputs(seed: int = 0) -> dict:
    streams_of = jax.random.split(jax.random.key(seed), 4)
    perturbation = draw_perturbation(jax.random.fold_in(streams_of[3], 71), 0)
    trajectory = gaussian(streams_of[1], (TRAJ, 3, 6, NX, NY), 0.3, 1.796875, ((0, 8), (3, 4)))
    step_order = jax.random.permutation(streams_of[2], TRAJ).astype(jnp.int32)
    return dict(perturbation=perturbation, trajectory=trajectory, step_order=step_order)


GRAVITY_TOP = 1.0
GRAVITY_LOW = 0.5
DEPTH_TOP = 1.0
DEPTH_LOW = 1.0
CORIOLIS = 0.3
TIME_STEP = 0.25

def diff_x(field):
    return 0.5 * (field[..., 2:, :] - field[..., :-2, :])

def diff_y(field):
    return 0.5 * (jnp.roll(field, -1, -1) - jnp.roll(field, 1, -1))

def trimmed(field, amount):
    return field[..., amount:field.shape[-2] - amount, :]

def tangent(base_state, tangent_state):
    dp_top = GRAVITY_TOP * (tangent_state[..., 0, :, :] + tangent_state[..., 3, :, :])
    dp_low = dp_top + GRAVITY_LOW * tangent_state[..., 3, :, :]
    results = []
    for layer_num, (mean_depth, pressure) in enumerate(((DEPTH_TOP, dp_top), (DEPTH_LOW, dp_low))):
        offset = 3 * layer_num
        base_depth = base_state[offset] + mean_depth
        base_xvel = base_state[offset + 1]
        base_yvel = base_state[offset + 2]
        pert_depth = tangent_state[..., offset, :, :]
        pert_xvel = tangent_state[..., offset + 1, :, :]
        pert_yvel = tangent_state[..., offset + 2, :, :]
        depth_rate = -diff_x(base_depth * pert_xvel + pert_depth * base_xvel) - trimmed(diff_y(base_depth * pert_yvel + pert_depth * base_yvel), 1)
        xvel_rate = -(trimmed(base_xvel, 1) * diff_x(pert_xvel) + trimmed(pert_xvel, 1) * diff_x(base_xvel)) - trimmed(base_yvel * diff_y(pert_xvel) + pert_yvel * diff_y(base_xvel), 1) + CORIOLIS * trimmed(pert_yvel, 1) - diff_x(pressure)
        yvel_rate = -(trimmed(base_xvel, 1) * diff_x(pert_yvel) + trimmed(pert_xvel, 1) * diff_x(base_yvel)) - trimmed(base_yvel * diff_y(pert_yvel) + pert_yvel * diff_y(base_yvel), 1) - CORIOLIS * trimmed(pert_xvel, 1) - trimmed(diff_y(pressure), 1)
        results += [depth_rate, xvel_rate, yvel_rate]
    return jnp.stack(results, axis=-3)

def combine(section_num, anchor, current, change):
    if section_num == 0:
        return current + TIME_STEP * change
    if section_num == 1:
        return 0.75 * anchor + 0.25 * (current + TIME_STEP * change)
    return anchor / 3.0 + 2.0 / 3.0 * (current + TIME_STEP * change)

def pad_rows(field):
    widths = [(0, 0)] * (field.ndim - 2) + [(1, 1), (0, 0)]
    return jnp.pad(field, widths, mode='wrap')

def reference(perturbation, trajectory, step_order):
    state = perturbation
    for step_num in range(STEPS):
        sections = trajectory[step_order[step_num]].astype(jnp.float32)
        padded_sections = pad_rows(sections)

        def advance(vector):
            current = vector
            for section_num in range(3):
                change = tangent(padded_sections[section_num], pad_rows(current))
                current = combine(section_num, vector, current, change)
            return current
        state = lax.map(advance, state)
    entries = 6 * state.shape[2] * state.shape[3]
    flat_cells = state.reshape(state.shape[0], -1)
    gram_matrix = jnp.dot(flat_cells.astype(jnp.float32), flat_cells.T.astype(jnp.float32), precision=lax.Precision.HIGHEST, preferred_element_type=jnp.float32) / entries
    lower_factor = jnp.linalg.cholesky(gram_matrix)
    ortho = jax.scipy.linalg.solve_triangular(lower_factor, flat_cells, lower=True)
    return (ortho.reshape(state.shape), jnp.transpose(lower_factor))
```

```python
import functools

import jax
import jax.numpy as jnp
from jax import lax
from jax.experimental import pallas as pl
from jax.experimental.pallas import tpu as pltpu
from jax.sharding import PartitionSpec as P

STEPS = 2
SECTIONS = 3
LAG = 4
RUN_LAG = 3
HALO = 8

GRAVITY_TOP = 1.0
GRAVITY_LOW = 0.5
DEPTH_TOP = 1.0
DEPTH_LOW = 1.0
CORIOLIS = 0.3
TIME_STEP = 0.25

MESH = pl.DeviceIdType.MESH
F32 = jnp.float32


def remote(src, dst, send, recv, target):
    return pltpu.make_async_remote_copy(
        src_ref=src, dst_ref=dst, send_sem=send, recv_sem=recv, device_id=target, device_id_type=MESH
    )


def await_bytes(ref, sem):
    pltpu.make_async_copy(ref, ref, sem).wait()


def diff_x(field):
    count = field.shape[0]
    return 0.5 * (pltpu.roll(field, count - 1, 0) - pltpu.roll(field, 1, 0))


def diff_y(field):
    count = field.shape[1]
    return 0.5 * (pltpu.roll(field, count - 1, 1) - pltpu.roll(field, 1, 1))


def tangent(base, state):
    dp_top = GRAVITY_TOP * (state[0] + state[3])
    dp_low = dp_top + GRAVITY_LOW * state[3]
    rates = []
    for layer, (mean_depth, pressure) in enumerate(((DEPTH_TOP, dp_top), (DEPTH_LOW, dp_low))):
        at = 3 * layer
        depth = base[at] + mean_depth
        u, v = base[at + 1], base[at + 2]
        dh, du, dv = state[at], state[at + 1], state[at + 2]
        rates.append(-diff_x(depth * du + dh * u) - diff_y(depth * dv + dh * v))
        rates.append(
            -(u * diff_x(du) + du * diff_x(u)) - (v * diff_y(du) + dv * diff_y(u))
            + CORIOLIS * dv - diff_x(pressure)
        )
        rates.append(
            -(u * diff_x(dv) + du * diff_x(v)) - (v * diff_y(dv) + dv * diff_y(v))
            - CORIOLIS * du - diff_y(pressure)
        )
    return rates


def slice_shape(n, fields, cols):
    lanes = cols // 128
    best = None
    for f in range(1, fields + 1):
        for l in range(1, lanes + 1):
            if fields % f or lanes % l or (fields // f) * (lanes // l) > n:
                continue
            if best is None or f * l < best[0] * best[1]:
                best = (f, l)
    return best


def whole_kernel(
    n, ns, entries, order_ref, traj_ref, pert_ref,
    out_ref, upper_ref,
    main, cand, in_up, in_dn, out_up, out_dn, pool, fresh, rims, anchor, work,
    x_ref, cols_ref, result, gspace, gvec, mine_s, mine_v,
    r_cand, r_up, r_dn, r_sec, r_pert, r_vec, r_gs, r_gv, r_back,
    s_cand, s_pert, s_up, s_dn, s_give, s_edge, s_vec, s_gs, s_gv, s_back,
):
    me = lax.axis_index("vec")
    tile = lax.axis_index("space")
    fields, rows, cols = pert_ref.shape
    half = fields // 2
    chunks = STEPS * SECTIONS * half
    parts = SECTIONS * half
    lines, places = n // 2, ns // 2
    side, line = lax.rem(me, 2), me // 2
    core, place = lax.rem(tile, 2), tile // 2
    flip = lax.rem(place, 2)

    def differs(a, b):
        return a + b - 2 * a * b

    home = differs(side, flip)
    stay = core == home
    away = core != home
    block = 2 * place + home
    vector = 2 * line + differs(core, flip)
    sibling = {"space": 2 * place + 1 - core}
    up_ok = line < lines - 1
    dn_ok = line > 0

    def worker(v, t):
        p = t // 2
        turn = lax.rem(p, 2)
        return {
            "vec": 2 * (v // 2) + differs(lax.rem(t, 2), turn),
            "space": 2 * p + differs(lax.rem(v, 2), turn),
        }

    barrier = pltpu.get_barrier_semaphore()
    near = sorted({0, 1 % places, places - 1})
    count = 0
    for across in range(2):
        for step in near:
            for c in range(2):
                if across == 0 and step == 0 and c == 0:
                    continue
                where = {
                    "vec": me + across * (1 - 2 * side),
                    "space": 2 * lax.rem(place + step, places) + lax.rem(core + c, 2),
                }
                pl.semaphore_signal(barrier, inc=1, device_id=where, device_id_type=MESH)
                count += 1

    @pl.when(up_ok)
    def _():
        pl.semaphore_signal(barrier, inc=1, device_id={"vec": me + 2}, device_id_type=MESH)

    @pl.when(dn_ok)
    def _():
        pl.semaphore_signal(barrier, inc=1, device_id={"vec": me - 2}, device_id_type=MESH)

    inner = pl.ds(HALO, rows)

    @pl.when(stay)
    def _():
        @pl.loop(0, parts)
        def _(p):
            k, f = lax.div(p, half), lax.rem(p, half)
            pltpu.make_async_copy(traj_ref.at[k, half * core + f], cand.at[0, p], r_cand.at[p]).start()

        pltpu.make_async_copy(pert_ref, anchor.at[:, inner], r_pert).start()

    pl.semaphore_wait(barrier, count + up_ok.astype(jnp.int32) + dn_ok.astype(jnp.int32))

    other = me + 1 - 2 * side

    @pl.when(stay)
    def _():
        @pl.loop(0, parts)
        def _(p):
            k, f = lax.div(p, half), lax.rem(p, half)
            remote(
                traj_ref.at[k, half * (1 - core) + f], cand.at[0, p], s_cand, r_cand.at[p], sibling
            ).start()

    @pl.when(away)
    def _():
        @pl.loop(0, parts)
        def _(p):
            k, f = lax.div(p, half), lax.rem(p, half)
            for c in range(2):
                remote(
                    traj_ref.at[k, half * c + f], cand.at[1, p], s_cand, r_cand.at[p],
                    {"vec": other, "space": 2 * place + c},
                ).start()

    next_tile = lax.rem(tile + 1, ns)
    prev_tile = lax.rem(tile + ns - 1, ns)
    remote(
        pert_ref.at[:, pl.ds(rows - HALO, HALO)], anchor.at[:, pl.ds(0, HALO)], s_pert, r_pert,
        worker(me, next_tile),
    ).start()
    remote(
        pert_ref.at[:, pl.ds(0, HALO)], anchor.at[:, pl.ds(HALO + rows, HALO)], s_pert, r_pert,
        worker(me, prev_tile),
    ).start()

    @pl.when(away)
    def _():
        remote(
            pert_ref, anchor.at[:, inner], s_pert, r_pert,
            {"vec": other, "space": 2 * place + 1 - core},
        ).start()

    def go_up(c):
        return remote(out_up.at[c], in_up.at[c], s_up, r_up.at[c], {"vec": me + 2})

    def go_dn(c):
        return remote(out_dn.at[c], in_dn.at[c], s_dn, r_dn.at[c], {"vec": me - 2})

    def owner_of(c):
        return jnp.where(c >= parts, order_ref[1], order_ref[0])

    def candidate(c):
        p = lax.rem(c, parts)
        return jnp.where(owner_of(c) == me, cand[0, p], cand[1, p])

    def inside(c):
        return (c >= 0) & (c < chunks)

    first_block = worker(vector, lax.rem(block + 1, ns))
    last_block = worker(vector, lax.rem(block + ns - 1, ns))
    own_layer = pl.ds(half * core, half)

    near_lag = LAG * jnp.minimum(line, lines - 1 - line)
    far_lag = LAG * jnp.maximum(line, lines - 1 - line)

    def advance(number, section, last):
        base = [main[number, f].astype(F32) for f in range(fields)]
        current = [work[f] for f in range(fields)]
        change = tangent(base, current)
        if last:
            keep, take = 1.0 / 3.0, 2.0 / 3.0
            mid = slice(HALO, HALO + rows)
            for f in range(fields):
                x_ref[f] = keep * anchor[f, mid] + take * (current[f][mid] + TIME_STEP * change[f][mid])
            return
        keep = jnp.where(section == 0, 0.0, jnp.where(section == 1, 0.75, 1.0 / 3.0)).astype(F32)
        take = jnp.where(section == 0, 1.0, jnp.where(section == 1, 0.25, 2.0 / 3.0)).astype(F32)
        for f in range(fields):
            work[f] = keep * anchor[f] + take * (current[f] + TIME_STEP * change[f])

        @pl.when(section == SECTIONS - 1)
        def _():
            anchor[...] = work[...]

    @pl.loop(0, LAG * (lines - 1) + chunks + RUN_LAG)
    def _(t):
        c_pair = t - near_lag
        c_up = t - LAG * line
        c_dn = t - LAG * (lines - 1 - line)
        c_fin = t - far_lag
        c_run = c_fin - RUN_LAG

        @pl.when((c_pair >= 0) & (c_pair < parts))
        def _():
            await_bytes(cand.at[:, c_pair], r_cand.at[c_pair])

        @pl.when(inside(c_up))
        def _():
            @pl.when(dn_ok)
            def _():
                go_up(c_up).wait_recv()

            @pl.when(up_ok)
            def _():
                here = lax.div(owner_of(c_up), 2) == line
                out_up[c_up] = jnp.where(here, candidate(c_up), in_up[c_up])
                go_up(c_up).start()

        @pl.when(inside(c_dn))
        def _():
            @pl.when(up_ok)
            def _():
                go_dn(c_dn).wait_recv()

            @pl.when(dn_ok)
            def _():
                here = lax.div(owner_of(c_dn), 2) == line
                out_dn[c_dn] = jnp.where(here, candidate(c_dn), in_dn[c_dn])
                go_dn(c_dn).start()

        @pl.when(inside(c_fin))
        def _():
            at = lax.div(owner_of(c_fin), 2)
            q, f = lax.div(c_fin, half), half * core + lax.rem(c_fin, half)
            main[q, f, inner] = jnp.where(
                at == line, candidate(c_fin), jnp.where(at < line, in_up[c_fin], in_dn[c_fin])
            )
            spot = main.at[q, f, inner]
            remote(spot, spot, s_give, r_sec.at[q], sibling).start()

            @pl.when(lax.rem(c_fin, half) == half - 1)
            def _():
                for c in range(2):
                    for target, src, dst in (
                        (first_block, rows, 0), (last_block, HALO, HALO + rows)
                    ):
                        remote(
                            main.at[q, own_layer, pl.ds(src, HALO)],
                            main.at[q, own_layer, pl.ds(dst, HALO)],
                            s_edge, r_sec.at[q],
                            {"vec": target["vec"], "space": 2 * (target["space"] // 2) + c},
                        ).start()

        @pl.when(c_run == half - 1)
        def _():
            await_bytes(anchor, r_pert)
            work[...] = anchor[...]

        @pl.when(inside(c_run) & (lax.rem(c_run, half) == half - 1))
        def _():
            number = lax.div(c_run, half)
            section = lax.rem(number, SECTIONS)
            await_bytes(fresh, r_sec.at[number])

            @pl.when(c_run < chunks - 1)
            def _():
                advance(number, section, False)

            @pl.when(c_run == chunks - 1)
            def _():
                advance(number, section, True)

    size_f, size_l = slice_shape(n, fields, cols)
    across = cols // (128 * size_l)
    slots = (fields // size_f) * across
    mine = 2 * line + core
    packed = n * n <= 128 and n % 8 == 0 and n * ns <= 64

    def slot(v):
        return n - 1 - v if packed else v

    def window(ref, j):
        f = pl.multiple_of(lax.div(j, across) * size_f, size_f)
        l = pl.multiple_of(lax.rem(j, across) * (128 * size_l), 128 * size_l)
        return ref.at[pl.ds(f, size_f), :, pl.ds(l, 128 * size_l)]

    def spread(d):
        to = lax.rem(mine + d, n)
        return to, {"vec": 2 * (to // 2) + side, "space": 2 * place + lax.rem(to, 2)}

    order = [d for d in sorted(range(1, n), key=lambda d: -min(d, n - d))]
    for d in order:
        to, where = spread(d)

        @pl.when(to < slots)
        def _():
            remote(window(x_ref, to), cols_ref.at[slot(vector)], s_vec, r_vec, where).start()

    @pl.when(mine < slots)
    def _():
        cols_ref[slot(vector)] = window(x_ref, mine)[...]

    @pl.when(stay)
    def _():
        await_bytes(pool.at[pl.ds(0, parts)], s_cand)
        await_bytes(anchor.at[:, pl.ds(0, 2 * HALO)], s_pert)

    @pl.when(away)
    def _():
        await_bytes(pool.at[pl.ds(0, 2 * parts)], s_cand)
        await_bytes(anchor, s_pert)

    await_bytes(out_up, s_give)
    await_bytes(rims, s_edge)

    @pl.when(up_ok)
    def _():
        await_bytes(out_up, s_up)

    @pl.when(dn_ok)
    def _():
        await_bytes(out_dn, s_dn)

    lanes = lax.broadcasted_iota(jnp.int32, (n, 128), 1)
    ranks = lax.broadcasted_iota(jnp.int32, (n, 128), 0)

    @pl.when(mine < slots)
    def _():
        await_bytes(cols_ref.at[pl.ds(0, n - 1)], r_vec)
        gram = jnp.zeros((n, 128), F32)
        for i in range(n):
            total = jnp.sum(cols_ref[...] * cols_ref[slot(i)][None], axis=(1, 2))
            if total.shape[-1] != 128:
                total = total.reshape(n, size_l, 128).sum(axis=1)
            gram = gram + jnp.where(lanes == i, jnp.sum(total, axis=1, keepdims=True), 0.0)
        mine_s[...] = gram

    @pl.when(mine >= slots)
    def _():
        mine_s[...] = jnp.zeros((n, 128), F32)

    if packed:
        row = jnp.sum(pltpu.roll(mine_s[...], 0, 1, stride=n, stride_axis=0), axis=0, keepdims=True)
        mine_v[...] = row
        rank = me * ns + tile
        reach = [(dv, ds) for dv in range(n) for ds in range(ns) if dv or ds]
        reach.sort(key=lambda e: -min(e[0], n - e[0]))
        for dv, ds in reach:
            where = {"vec": lax.rem(me + dv, n), "space": lax.rem(tile + ds, ns)}
            remote(mine_v, gvec.at[rank], s_gv, r_gv, where).start()
        gvec[rank] = row
        await_bytes(gvec.at[pl.ds(0, n * ns - 1)], r_gv)
        row = gvec[0]
        for i in range(1, n * ns):
            row = row + gvec[i]
        gram = pltpu.roll(jnp.broadcast_to(row, (n, 128)), 128 - n * (n - 1), 1, stride=n, stride_axis=0)
    else:
        for d in range(1, ns):
            to = lax.rem(tile + d, ns)
            remote(mine_s, gspace.at[tile], s_gs, r_gs, {"space": to}).start()
        gspace[tile] = mine_s[...]
        await_bytes(gspace.at[pl.ds(0, ns - 1)], r_gs)
        gram = gspace[0]
        for i in range(1, ns):
            gram = gram + gspace[i]
        mine_v[...] = gram
        for d in range(1, n):
            to = lax.rem(me + d, n)
            remote(mine_v, gvec.at[me], s_gv, r_gv, {"vec": to}).start()
        gvec[me] = gram
        await_bytes(gvec.at[pl.ds(0, n - 1)], r_gv)
        gram = gvec[0]
        for i in range(1, n):
            gram = gram + gvec[i]

    a = jnp.where(lanes < n, gram / entries, 0.0) + jnp.where(lanes == ranks + n, 1.0, 0.0)
    for k in range(n):
        pivot_row = a[k : k + 1, :]
        column = jnp.sum(jnp.where(lanes == k, a, 0.0), axis=1, keepdims=True)
        factor = jnp.where(ranks[:, :1] > k, column / column[k : k + 1, :], 0.0)
        a = a - factor * pivot_row
    diagonal = jnp.sum(jnp.where(lanes == ranks, a, 0.0), axis=1, keepdims=True)
    a = a / jnp.sqrt(diagonal)
    upper_ref[...] = jnp.where(lanes >= ranks, a, 0.0)

    @pl.when(mine < slots)
    def _():
        for i in range(n):
            total = a[i : i + 1, n : n + 1][None] * cols_ref[slot(0)]
            for j in range(1, i + 1):
                total = total + a[i : i + 1, n + j : n + j + 1][None] * cols_ref[slot(j)]
            result[i] = total

            @pl.when((me != i) | away)
            def _():
                remote(
                    result.at[i], window(out_ref, mine), s_back, r_back, {"vec": i, "space": block}
                ).start()

            @pl.when((me == i) & stay)
            def _():
                window(out_ref, mine)[...] = total

    def drain(several, fewer, sem):
        @pl.when(fewer)
        def _():
            await_bytes(result.at[pl.ds(0, several - 1)], sem)

        @pl.when(jnp.logical_not(fewer))
        def _():
            await_bytes(result.at[pl.ds(0, several)], sem)

    drain(slots, stay & (mine < slots), r_back)
    drain(slots, mine < slots, s_vec)

    @pl.when(mine < slots)
    def _():
        drain(n, stay, s_back)

    if packed:
        await_bytes(gvec.at[pl.ds(0, n * ns - 1)], s_gv)
    else:
        await_bytes(gspace.at[pl.ds(0, ns - 1)], s_gs)
        await_bytes(gvec.at[pl.ds(0, n - 1)], s_gv)


def body(n, ns, perturbation, trajectory, step_order):
    pert, traj = perturbation[0], trajectory[0]
    fields, rows, cols = pert.shape
    sections = traj.shape[0]
    chunks, bf = STEPS * sections * (fields // 2), traj.dtype
    packed = n * n <= 128 and n % 8 == 0 and n * ns <= 64
    size_f, size_l = slice_shape(n, fields, cols)
    vmem = pl.BlockSpec(memory_space=pltpu.VMEM)
    hbm = pl.BlockSpec(memory_space=pl.ANY)
    piece = pltpu.VMEM((chunks, rows, cols), bf)
    full = pltpu.VMEM((fields, rows + 2 * HALO, cols), F32)
    slices = pltpu.VMEM((n, size_f, rows, 128 * size_l), F32)
    small = pltpu.VMEM((n, 128), F32)
    dma, one = pltpu.SemaphoreType.DMA, pltpu.SemaphoreType.DMA(())
    out, upper = pl.pallas_call(
        functools.partial(whole_kernel, n, ns, float(fields * rows * cols * ns)),
        out_shape=(
            jax.ShapeDtypeStruct(pert.shape, F32),
            jax.ShapeDtypeStruct((n, 128), F32),
        ),
        in_specs=[pl.BlockSpec(memory_space=pltpu.SMEM), hbm, hbm],
        out_specs=(vmem, vmem),
        scratch_shapes=[
            pltpu.VMEM((STEPS * sections, fields, rows + 2 * HALO, cols), bf),
            pltpu.VMEM((2, sections * (fields // 2), rows, cols), bf),
            piece, piece, piece, piece, piece,
            pltpu.VMEM((fields // 2, rows + 4 * HALO, cols), bf),
            pltpu.VMEM((STEPS * sections, fields, 2 * HALO, cols), bf),
            full, full,
            pltpu.VMEM(pert.shape, F32), slices, slices,
            pltpu.VMEM((ns, n, 128), F32),
            pltpu.VMEM((n * ns, 1, 128) if packed else (n, n, 128), F32),
            small,
            pltpu.VMEM((1, 128), F32) if packed else small,
            dma((sections * (fields // 2),)), dma((chunks,)), dma((chunks,)), dma((STEPS * sections,)),
            one, one, one, one, one,
            one, one, one, one, one, one, one, one, one, one,
        ],
        compiler_params=pltpu.CompilerParams(collective_id=0, has_side_effects=True),
        name="whole",
    )(step_order, traj, pert)

    def finish(back_ref, upper_ref, out_ref, factor_ref):
        out_ref[...] = back_ref[...]
        factor_ref[...] = upper_ref[:, :n]

    out, factor = pl.pallas_call(
        finish,
        out_shape=(jax.ShapeDtypeStruct(pert.shape, F32), jax.ShapeDtypeStruct((n, n), F32)),
        in_specs=[vmem, vmem],
        out_specs=(vmem, vmem),
        name="finish",
    )(out, upper)
    return out[None], factor


def solution(mesh):
    n, ns = mesh.shape["vec"], mesh.shape["space"]
    in_specs = (P("vec", None, "space", None), P("vec", None, None, "space", None), P())
    out_specs = (P("vec", None, "space", None), P())
    return jax.shard_map(
        functools.partial(body, n, ns), mesh=mesh, in_specs=in_specs, out_specs=out_specs, check_vma=False
    )
```

```python
import functools

import jax
import jax.numpy as jnp
from jax import lax
from jax.experimental import pallas as pl
from jax.experimental.pallas import tpu as pltpu
from jax.sharding import PartitionSpec as P

STEPS = 2
SECTIONS = 3
LAG = 6
RUN_LAG = 7
HALO = 8

GRAVITY_TOP = 1.0
GRAVITY_LOW = 0.5
DEPTH_TOP = 1.0
DEPTH_LOW = 1.0
CORIOLIS = 0.3
TIME_STEP = 0.25

MESH = pl.DeviceIdType.MESH
F32 = jnp.float32


def remote(src, dst, send, recv, target):
    return pltpu.make_async_remote_copy(
        src_ref=src, dst_ref=dst, send_sem=send, recv_sem=recv, device_id=target, device_id_type=MESH
    )


def await_bytes(ref, sem):
    pltpu.make_async_copy(ref, ref, sem).wait()


def diff_x(field):
    count = field.shape[0]
    return 0.5 * (pltpu.roll(field, count - 1, 0) - pltpu.roll(field, 1, 0))


def diff_y(field):
    count = field.shape[1]
    return 0.5 * (pltpu.roll(field, count - 1, 1) - pltpu.roll(field, 1, 1))


def tangent(base, state):
    dp_top = GRAVITY_TOP * (state[0] + state[3])
    dp_low = dp_top + GRAVITY_LOW * state[3]
    rates = []
    for layer, (mean_depth, pressure) in enumerate(((DEPTH_TOP, dp_top), (DEPTH_LOW, dp_low))):
        at = 3 * layer
        depth = base[at] + mean_depth
        u, v = base[at + 1], base[at + 2]
        dh, du, dv = state[at], state[at + 1], state[at + 2]
        rates.append(-diff_x(depth * du + dh * u) - diff_y(depth * dv + dh * v))
        rates.append(
            -(u * diff_x(du) + du * diff_x(u)) - (v * diff_y(du) + dv * diff_y(u))
            + CORIOLIS * dv - diff_x(pressure)
        )
        rates.append(
            -(u * diff_x(dv) + du * diff_x(v)) - (v * diff_y(dv) + dv * diff_y(v))
            - CORIOLIS * du - diff_y(pressure)
        )
    return rates


def slice_shape(n, fields, cols):
    lanes = cols // 128
    best = None
    for f in range(1, fields + 1):
        for l in range(1, lanes + 1):
            if fields % f or lanes % l or (fields // f) * (lanes // l) > n:
                continue
            if best is None or f * l < best[0] * best[1]:
                best = (f, l)
    return best


def whole_kernel(
    n, ns, entries, order_ref, traj_ref, pert_ref,
    out_ref, upper_ref,
    main, cand, in_up, in_dn, out_up, out_dn, pool, fresh, rims, anchor, work,
    x_ref, cols_ref, result, gspace, gvec, mine_s, mine_v,
    r_cand, r_up, r_dn, r_sec, r_pert, r_vec, r_gs, r_gv, r_back,
    s_cand, s_pert, s_up, s_dn, s_give, s_edge, s_vec, s_gs, s_gv, s_back,
):
    me = lax.axis_index("vec")
    tile = lax.axis_index("space")
    fields, rows, cols = pert_ref.shape
    half = fields // 2
    chunks = STEPS * SECTIONS * half
    parts = SECTIONS * half
    lines, places = n // 2, ns // 2
    side, line = lax.rem(me, 2), me // 2
    core, place = lax.rem(tile, 2), tile // 2
    flip = lax.rem(place, 2)

    def differs(a, b):
        return a + b - 2 * a * b

    home = differs(side, flip)
    stay = core == home
    away = core != home
    block = 2 * place + home
    vector = 2 * line + differs(core, flip)
    sibling = {"space": 2 * place + 1 - core}
    up_ok = line < lines - 1
    dn_ok = line > 0

    def worker(v, t):
        p = t // 2
        turn = lax.rem(p, 2)
        return {
            "vec": 2 * (v // 2) + differs(lax.rem(t, 2), turn),
            "space": 2 * p + differs(lax.rem(v, 2), turn),
        }

    barrier = pltpu.get_barrier_semaphore()
    near = sorted({0, 1 % places, places - 1})
    count = 0
    for across in range(2):
        for step in near:
            for c in range(2):
                if across == 0 and step == 0 and c == 0:
                    continue
                where = {
                    "vec": me + across * (1 - 2 * side),
                    "space": 2 * lax.rem(place + step, places) + lax.rem(core + c, 2),
                }
                pl.semaphore_signal(barrier, inc=1, device_id=where, device_id_type=MESH)
                count += 1

    @pl.when(up_ok)
    def _():
        pl.semaphore_signal(barrier, inc=1, device_id={"vec": me + 2}, device_id_type=MESH)

    @pl.when(dn_ok)
    def _():
        pl.semaphore_signal(barrier, inc=1, device_id={"vec": me - 2}, device_id_type=MESH)

    inner = pl.ds(HALO, rows)

    @pl.when(stay)
    def _():
        @pl.loop(0, parts)
        def _(p):
            k, f = lax.div(p, half), lax.rem(p, half)
            pltpu.make_async_copy(traj_ref.at[k, half * core + f], cand.at[0, p], r_cand.at[p]).start()

        pltpu.make_async_copy(pert_ref, anchor.at[:, inner], r_pert).start()

    pl.semaphore_wait(barrier, count + up_ok.astype(jnp.int32) + dn_ok.astype(jnp.int32))

    other = me + 1 - 2 * side

    @pl.when(stay)
    def _():
        @pl.loop(0, parts)
        def _(p):
            k, f = lax.div(p, half), lax.rem(p, half)
            remote(
                traj_ref.at[k, half * (1 - core) + f], cand.at[0, p], s_cand, r_cand.at[p], sibling
            ).start()

    @pl.when(away)
    def _():
        @pl.loop(0, parts)
        def _(p):
            k, f = lax.div(p, half), lax.rem(p, half)
            for c in range(2):
                remote(
                    traj_ref.at[k, half * c + f], cand.at[1, p], s_cand, r_cand.at[p],
                    {"vec": other, "space": 2 * place + c},
                ).start()

    next_tile = lax.rem(tile + 1, ns)
    prev_tile = lax.rem(tile + ns - 1, ns)
    remote(
        pert_ref.at[:, pl.ds(rows - HALO, HALO)], anchor.at[:, pl.ds(0, HALO)], s_pert, r_pert,
        worker(me, next_tile),
    ).start()
    remote(
        pert_ref.at[:, pl.ds(0, HALO)], anchor.at[:, pl.ds(HALO + rows, HALO)], s_pert, r_pert,
        worker(me, prev_tile),
    ).start()

    @pl.when(away)
    def _():
        remote(
            pert_ref, anchor.at[:, inner], s_pert, r_pert,
            {"vec": other, "space": 2 * place + 1 - core},
        ).start()

    def go_up(c):
        return remote(out_up.at[c], in_up.at[c], s_up, r_up.at[c], {"vec": me + 2})

    def go_dn(c):
        return remote(out_dn.at[c], in_dn.at[c], s_dn, r_dn.at[c], {"vec": me - 2})

    def owner_of(c):
        return jnp.where(c >= parts, order_ref[1], order_ref[0])

    def candidate(c):
        p = lax.rem(c, parts)
        return jnp.where(owner_of(c) == me, cand[0, p], cand[1, p])

    def inside(c):
        return (c >= 0) & (c < chunks)

    first_block = worker(vector, lax.rem(block + 1, ns))
    last_block = worker(vector, lax.rem(block + ns - 1, ns))
    own_layer = pl.ds(half * core, half)

    near_lag = LAG * jnp.minimum(line, lines - 1 - line)
    far_lag = LAG * jnp.maximum(line, lines - 1 - line)

    def advance(number, section, last):
        base = [main[number, f].astype(F32) for f in range(fields)]
        current = [work[f] for f in range(fields)]
        change = tangent(base, current)
        if last:
            keep, take = 1.0 / 3.0, 2.0 / 3.0
            mid = slice(HALO, HALO + rows)
            for f in range(fields):
                x_ref[f] = keep * anchor[f, mid] + take * (current[f][mid] + TIME_STEP * change[f][mid])
            return
        keep = jnp.where(section == 0, 0.0, jnp.where(section == 1, 0.75, 1.0 / 3.0)).astype(F32)
        take = jnp.where(section == 0, 1.0, jnp.where(section == 1, 0.25, 2.0 / 3.0)).astype(F32)
        for f in range(fields):
            work[f] = keep * anchor[f] + take * (current[f] + TIME_STEP * change[f])

        @pl.when(section == SECTIONS - 1)
        def _():
            anchor[...] = work[...]

    @pl.loop(0, LAG * (lines - 1) + chunks + RUN_LAG)
    def _(t):
        c_pair = t - near_lag
        c_up = t - LAG * line
        c_dn = t - LAG * (lines - 1 - line)
        c_fin = t - far_lag
        c_run = c_fin - RUN_LAG

        @pl.when((c_pair >= 0) & (c_pair < parts))
        def _():
            await_bytes(cand.at[:, c_pair], r_cand.at[c_pair])

        @pl.when(inside(c_up))
        def _():
            @pl.when(dn_ok)
            def _():
                go_up(c_up).wait_recv()

            @pl.when(up_ok)
            def _():
                here = lax.div(owner_of(c_up), 2) == line
                out_up[c_up] = jnp.where(here, candidate(c_up), in_up[c_up])
                go_up(c_up).start()

        @pl.when(inside(c_dn))
        def _():
            @pl.when(up_ok)
            def _():
                go_dn(c_dn).wait_recv()

            @pl.when(dn_ok)
            def _():
                here = lax.div(owner_of(c_dn), 2) == line
                out_dn[c_dn] = jnp.where(here, candidate(c_dn), in_dn[c_dn])
                go_dn(c_dn).start()

        @pl.when(inside(c_fin))
        def _():
            at = lax.div(owner_of(c_fin), 2)
            q, f = lax.div(c_fin, half), half * core + lax.rem(c_fin, half)
            main[q, f, inner] = jnp.where(
                at == line, candidate(c_fin), jnp.where(at < line, in_up[c_fin], in_dn[c_fin])
            )
            spot = main.at[q, f, inner]
            remote(spot, spot, s_give, r_sec.at[q], sibling).start()

            @pl.when(lax.rem(c_fin, half) == half - 1)
            def _():
                for c in range(2):
                    for target, src, dst in (
                        (first_block, rows, 0), (last_block, HALO, HALO + rows)
                    ):
                        remote(
                            main.at[q, own_layer, pl.ds(src, HALO)],
                            main.at[q, own_layer, pl.ds(dst, HALO)],
                            s_edge, r_sec.at[q],
                            {"vec": target["vec"], "space": 2 * (target["space"] // 2) + c},
                        ).start()

        @pl.when(c_run == half - 1)
        def _():
            await_bytes(anchor, r_pert)
            work[...] = anchor[...]

        @pl.when(inside(c_run) & (lax.rem(c_run, half) == half - 1))
        def _():
            number = lax.div(c_run, half)
            section = lax.rem(number, SECTIONS)
            await_bytes(fresh, r_sec.at[number])

            @pl.when(c_run < chunks - 1)
            def _():
                advance(number, section, False)

            @pl.when(c_run == chunks - 1)
            def _():
                advance(number, section, True)

    size_f, size_l = slice_shape(n, fields, cols)
    across = cols // (128 * size_l)
    slots = (fields // size_f) * across
    mine = 2 * line + core
    packed = n * n <= 128 and n % 8 == 0 and n * ns <= 64

    def slot(v):
        return n - 1 - v if packed else v

    def window(ref, j):
        f = pl.multiple_of(lax.div(j, across) * size_f, size_f)
        l = pl.multiple_of(lax.rem(j, across) * (128 * size_l), 128 * size_l)
        return ref.at[pl.ds(f, size_f), :, pl.ds(l, 128 * size_l)]

    def spread(d):
        to = lax.rem(mine + d, n)
        return to, {"vec": 2 * (to // 2) + side, "space": 2 * place + lax.rem(to, 2)}

    order = [d for d in sorted(range(1, n), key=lambda d: -min(d, n - d))]
    for d in order:
        to, where = spread(d)

        @pl.when(to < slots)
        def _():
            remote(window(x_ref, to), cols_ref.at[slot(vector)], s_vec, r_vec, where).start()

    @pl.when(mine < slots)
    def _():
        cols_ref[slot(vector)] = window(x_ref, mine)[...]

    @pl.when(stay)
    def _():
        await_bytes(pool.at[pl.ds(0, parts)], s_cand)
        await_bytes(anchor.at[:, pl.ds(0, 2 * HALO)], s_pert)

    @pl.when(away)
    def _():
        await_bytes(pool.at[pl.ds(0, 2 * parts)], s_cand)
        await_bytes(anchor, s_pert)

    await_bytes(out_up, s_give)
    await_bytes(rims, s_edge)

    @pl.when(up_ok)
    def _():
        await_bytes(out_up, s_up)

    @pl.when(dn_ok)
    def _():
        await_bytes(out_dn, s_dn)

    lanes = lax.broadcasted_iota(jnp.int32, (n, 128), 1)
    ranks = lax.broadcasted_iota(jnp.int32, (n, 128), 0)

    @pl.when(mine < slots)
    def _():
        await_bytes(cols_ref.at[pl.ds(0, n - 1)], r_vec)
        gram = jnp.zeros((n, 128), F32)
        for i in range(n):
            total = jnp.sum(cols_ref[...] * cols_ref[slot(i)][None], axis=(1, 2))
            if total.shape[-1] != 128:
                total = total.reshape(n, size_l, 128).sum(axis=1)
            gram = gram + jnp.where(lanes == i, jnp.sum(total, axis=1, keepdims=True), 0.0)
        mine_s[...] = gram

    @pl.when(mine >= slots)
    def _():
        mine_s[...] = jnp.zeros((n, 128), F32)

    if packed:
        row = jnp.sum(pltpu.roll(mine_s[...], 0, 1, stride=n, stride_axis=0), axis=0, keepdims=True)
        mine_v[...] = row
        rank = me * ns + tile
        reach = [(dv, ds) for dv in range(n) for ds in range(ns) if dv or ds]
        reach.sort(key=lambda e: -min(e[0], n - e[0]))
        for dv, ds in reach:
            where = {"vec": lax.rem(me + dv, n), "space": lax.rem(tile + ds, ns)}
            remote(mine_v, gvec.at[rank], s_gv, r_gv, where).start()
        gvec[rank] = row
        await_bytes(gvec.at[pl.ds(0, n * ns - 1)], r_gv)
        row = gvec[0]
        for i in range(1, n * ns):
            row = row + gvec[i]
        gram = pltpu.roll(jnp.broadcast_to(row, (n, 128)), 128 - n * (n - 1), 1, stride=n, stride_axis=0)
    else:
        for d in range(1, ns):
            to = lax.rem(tile + d, ns)
            remote(mine_s, gspace.at[tile], s_gs, r_gs, {"space": to}).start()
        gspace[tile] = mine_s[...]
        await_bytes(gspace.at[pl.ds(0, ns - 1)], r_gs)
        gram = gspace[0]
        for i in range(1, ns):
            gram = gram + gspace[i]
        mine_v[...] = gram
        for d in range(1, n):
            to = lax.rem(me + d, n)
            remote(mine_v, gvec.at[me], s_gv, r_gv, {"vec": to}).start()
        gvec[me] = gram
        await_bytes(gvec.at[pl.ds(0, n - 1)], r_gv)
        gram = gvec[0]
        for i in range(1, n):
            gram = gram + gvec[i]

    a = jnp.where(lanes < n, gram / entries, 0.0) + jnp.where(lanes == ranks + n, 1.0, 0.0)
    for k in range(n):
        pivot_row = a[k : k + 1, :]
        column = jnp.sum(jnp.where(lanes == k, a, 0.0), axis=1, keepdims=True)
        factor = jnp.where(ranks[:, :1] > k, column / column[k : k + 1, :], 0.0)
        a = a - factor * pivot_row
    diagonal = jnp.sum(jnp.where(lanes == ranks, a, 0.0), axis=1, keepdims=True)
    a = a / jnp.sqrt(diagonal)
    upper_ref[...] = jnp.where(lanes >= ranks, a, 0.0)[:, :n]

    @pl.when(mine < slots)
    def _():
        for i in range(n):
            total = a[i : i + 1, n : n + 1][None] * cols_ref[slot(0)]
            for j in range(1, i + 1):
                total = total + a[i : i + 1, n + j : n + j + 1][None] * cols_ref[slot(j)]
            result[i] = total

        for d in range(n):
            i = lax.rem(vector + n // 2 + d, n)

            @pl.when((me != i) | away)
            def _():
                remote(
                    result.at[i], window(out_ref, mine), s_back, r_back, {"vec": i, "space": block}
                ).start()

        @pl.when(stay)
        def _():
            window(out_ref, mine)[...] = result[me]

    def drain(several, fewer, sem):
        @pl.when(fewer)
        def _():
            await_bytes(result.at[pl.ds(0, several - 1)], sem)

        @pl.when(jnp.logical_not(fewer))
        def _():
            await_bytes(result.at[pl.ds(0, several)], sem)

    drain(slots, stay & (mine < slots), r_back)
    drain(slots, mine < slots, s_vec)

    @pl.when(mine < slots)
    def _():
        drain(n, stay, s_back)

    if packed:
        await_bytes(gvec.at[pl.ds(0, n * ns - 1)], s_gv)
    else:
        await_bytes(gspace.at[pl.ds(0, ns - 1)], s_gs)
        await_bytes(gvec.at[pl.ds(0, n - 1)], s_gv)


def body(n, ns, perturbation, trajectory, step_order):
    pert, traj = perturbation[0], trajectory[0]
    fields, rows, cols = pert.shape
    sections = traj.shape[0]
    chunks, bf = STEPS * sections * (fields // 2), traj.dtype
    packed = n * n <= 128 and n % 8 == 0 and n * ns <= 64
    size_f, size_l = slice_shape(n, fields, cols)
    vmem = pl.BlockSpec(memory_space=pltpu.VMEM)
    hbm = pl.BlockSpec(memory_space=pl.ANY)
    piece = pltpu.VMEM((chunks, rows, cols), bf)
    full = pltpu.VMEM((fields, rows + 2 * HALO, cols), F32)
    slices = pltpu.VMEM((n, size_f, rows, 128 * size_l), F32)
    small = pltpu.VMEM((n, 128), F32)
    dma, one = pltpu.SemaphoreType.DMA, pltpu.SemaphoreType.DMA(())
    out, upper = pl.pallas_call(
        functools.partial(whole_kernel, n, ns, float(fields * rows * cols * ns)),
        out_shape=(pltpu.VMEM(pert.shape, F32), pltpu.VMEM((n, n), F32)),
        in_specs=[pl.BlockSpec(memory_space=pltpu.SMEM), hbm, hbm],
        out_specs=(vmem, vmem),
        scratch_shapes=[
            pltpu.VMEM((STEPS * sections, fields, rows + 2 * HALO, cols), bf),
            pltpu.VMEM((2, sections * (fields // 2), rows, cols), bf),
            piece, piece, piece, piece, piece,
            pltpu.VMEM((fields // 2, rows + 4 * HALO, cols), bf),
            pltpu.VMEM((STEPS * sections, fields, 2 * HALO, cols), bf),
            full, full,
            pltpu.VMEM(pert.shape, F32), slices, slices,
            pltpu.VMEM((ns, n, 128), F32),
            pltpu.VMEM((n * ns, 1, 128) if packed else (n, n, 128), F32),
            small,
            pltpu.VMEM((1, 128), F32) if packed else small,
            dma((sections * (fields // 2),)), dma((chunks,)), dma((chunks,)), dma((STEPS * sections,)),
            one, one, one, one, one,
            one, one, one, one, one, one, one, one, one, one,
        ],
        compiler_params=pltpu.CompilerParams(collective_id=0, has_side_effects=True),
        name="whole",
    )(step_order, traj, pert)

    def finish(back_ref, upper_ref, out_ref, factor_ref, sems):
        copies = [
            pltpu.make_async_copy(back_ref, out_ref, sems.at[0]),
            pltpu.make_async_copy(upper_ref, factor_ref, sems.at[1]),
        ]
        for copy in copies:
            copy.start()
        for copy in copies:
            copy.wait()

    out, factor = pl.pallas_call(
        finish,
        out_shape=(jax.ShapeDtypeStruct(pert.shape, F32), jax.ShapeDtypeStruct((n, n), F32)),
        in_specs=[vmem, vmem],
        out_specs=(hbm, hbm),
        scratch_shapes=[dma((2,))],
        name="finish",
    )(
        pltpu.with_memory_space_constraint(out, pltpu.VMEM),
        pltpu.with_memory_space_constraint(upper, pltpu.VMEM),
    )
    return out[None], factor


def solution(mesh):
    n, ns = mesh.shape["vec"], mesh.shape["space"]
    in_specs = (P("vec", None, "space", None), P("vec", None, None, "space", None), P())
    out_specs = (P("vec", None, "space", None), P())
    return jax.shard_map(
        functools.partial(body, n, ns), mesh=mesh, in_specs=in_specs, out_specs=out_specs, check_vma=False
    )
```

```python
import functools

import jax
import jax.numpy as jnp
from jax import lax
from jax.experimental import pallas as pl
from jax.experimental.pallas import tpu as pltpu
from jax.sharding import PartitionSpec as P

STEPS = 2
SECTIONS = 3
LAG = 6
RUN_LAG_END = 8
RUN_LAG_MID = 15
HALO = 8

GRAVITY_TOP = 1.0
GRAVITY_LOW = 0.5
DEPTH_TOP = 1.0
DEPTH_LOW = 1.0
CORIOLIS = 0.3
TIME_STEP = 0.25

MESH = pl.DeviceIdType.MESH
F32 = jnp.float32


def remote(src, dst, send, recv, target):
    return pltpu.make_async_remote_copy(
        src_ref=src, dst_ref=dst, send_sem=send, recv_sem=recv, device_id=target, device_id_type=MESH
    )


def await_bytes(ref, sem):
    pltpu.make_async_copy(ref, ref, sem).wait()


def diff_x(field):
    count = field.shape[0]
    return 0.5 * (pltpu.roll(field, count - 1, 0) - pltpu.roll(field, 1, 0))


def diff_y(field):
    count = field.shape[1]
    return 0.5 * (pltpu.roll(field, count - 1, 1) - pltpu.roll(field, 1, 1))


def tangent(layer, base, state, top, low):
    pressure = GRAVITY_TOP * (top + low)
    if layer:
        pressure = pressure + GRAVITY_LOW * low
    depth = base[0] + (DEPTH_TOP, DEPTH_LOW)[layer]
    u, v = base[1], base[2]
    dh, du, dv = state
    return [
        -diff_x(depth * du + dh * u) - diff_y(depth * dv + dh * v),
        -(u * diff_x(du) + du * diff_x(u)) - (v * diff_y(du) + dv * diff_y(u))
        + CORIOLIS * dv - diff_x(pressure),
        -(u * diff_x(dv) + du * diff_x(v)) - (v * diff_y(dv) + dv * diff_y(v))
        - CORIOLIS * du - diff_y(pressure),
    ]


def slice_shape(n, fields, cols):
    lanes = cols // 128
    best = None
    for f in range(1, fields + 1):
        for l in range(1, lanes + 1):
            if fields % f or lanes % l or (fields // f) * (lanes // l) > n:
                continue
            if best is None or f * l < best[0] * best[1]:
                best = (f, l)
    return best


def whole_kernel(
    n, ns, entries, order_ref, traj_ref, pert_ref,
    out_ref, upper_ref,
    main, cand, in_up, in_dn, out_up, out_dn, pool, fresh, rims, anchor, work,
    x_ref, cols_ref, result, gspace, gvec, mine_s, mine_v,
    r_cand, r_up, r_dn, r_sec, r_pert, r_side, r_vec, r_gs, r_gv, r_back,
    s_cand, s_pert, s_side, s_up, s_dn, s_give, s_edge, s_vec, s_gs, s_gv, s_back,
):
    me = lax.axis_index("vec")
    tile = lax.axis_index("space")
    fields, rows, cols = pert_ref.shape
    half = fields // 2
    chunks = STEPS * SECTIONS * half
    parts = SECTIONS * half
    lines, places = n // 2, ns // 2
    side, line = lax.rem(me, 2), me // 2
    core, place = lax.rem(tile, 2), tile // 2
    flip = lax.rem(place, 2)

    def differs(a, b):
        return a + b - 2 * a * b

    home = differs(side, flip)
    stay = core == home
    away = core != home
    block = 2 * place + home
    vector = 2 * line + differs(core, flip)
    sibling = {"space": 2 * place + 1 - core}
    up_ok = line < lines - 1
    dn_ok = line > 0

    def worker(v, t):
        p = t // 2
        turn = lax.rem(p, 2)
        return {
            "vec": 2 * (v // 2) + differs(lax.rem(t, 2), turn),
            "space": 2 * p + differs(lax.rem(v, 2), turn),
        }

    barrier = pltpu.get_barrier_semaphore()
    near = sorted({0, 1 % places, places - 1})
    count = 0
    for across in range(2):
        for step in near:
            for c in range(2):
                if (across == 0 and step == 0 and c == 0) or (across and step):
                    continue
                where = {
                    "vec": me + across * (1 - 2 * side),
                    "space": 2 * lax.rem(place + step, places) + lax.rem(core + c, 2),
                }
                pl.semaphore_signal(barrier, inc=1, device_id=where, device_id_type=MESH)
                count += 1

    @pl.when(up_ok)
    def _():
        pl.semaphore_signal(barrier, inc=1, device_id={"vec": me + 2}, device_id_type=MESH)

    @pl.when(dn_ok)
    def _():
        pl.semaphore_signal(barrier, inc=1, device_id={"vec": me - 2}, device_id_type=MESH)

    inner = pl.ds(HALO, rows)

    @pl.when(stay)
    def _():
        @pl.loop(0, parts)
        def _(p):
            k, f = lax.div(p, half), lax.rem(p, half)
            pltpu.make_async_copy(traj_ref.at[k, half * core + f], cand.at[0, p], r_cand.at[p]).start()

        pltpu.make_async_copy(pert_ref, anchor.at[:, inner], r_pert).start()

    pl.semaphore_wait(barrier, count + up_ok.astype(jnp.int32) + dn_ok.astype(jnp.int32))

    other = me + 1 - 2 * side

    @pl.when(stay)
    def _():
        @pl.loop(0, parts)
        def _(p):
            k, f = lax.div(p, half), lax.rem(p, half)
            remote(
                traj_ref.at[k, half * (1 - core) + f], cand.at[0, p], s_cand, r_cand.at[p], sibling
            ).start()

    @pl.when(away)
    def _():
        @pl.loop(0, parts)
        def _(p):
            k, f = lax.div(p, half), lax.rem(p, half)
            for c in range(2):
                remote(
                    traj_ref.at[k, half * c + f], cand.at[1, p], s_cand, r_cand.at[p],
                    {"vec": other, "space": 2 * place + c},
                ).start()

    @pl.when(away)
    def _():
        remote(
            pert_ref, anchor.at[:, inner], s_pert, r_pert,
            {"vec": other, "space": 2 * place + 1 - core},
        ).start()

    def go_up(c):
        return remote(out_up.at[c], in_up.at[c], s_up, r_up.at[c], {"vec": me + 2})

    def go_dn(c):
        return remote(out_dn.at[c], in_dn.at[c], s_dn, r_dn.at[c], {"vec": me - 2})

    def owner_of(c):
        return jnp.where(c >= parts, order_ref[1], order_ref[0])

    def candidate(c):
        p = lax.rem(c, parts)
        return jnp.where(owner_of(c) == me, cand[0, p], cand[1, p])

    def inside(c):
        return (c >= 0) & (c < chunks)

    first_block = worker(vector, lax.rem(block + 1, ns))
    last_block = worker(vector, lax.rem(block + ns - 1, ns))
    own_layer = pl.ds(half * core, half)

    run_lag = jnp.where(up_ok & dn_ok, RUN_LAG_MID, RUN_LAG_END)
    near_lag = LAG * jnp.minimum(line, lines - 1 - line)
    far_lag = LAG * jnp.maximum(line, lines - 1 - line)

    def rates(number, layer):
        now = lax.rem(number, 2)
        at = half * layer
        base = [main[number, at + f].astype(F32) for f in range(half)]
        state = [work[now, at + f] for f in range(half)]
        top = state[0] if layer == 0 else work[now, 0]
        low = state[0] if layer == 1 else work[now, half]
        return state, tangent(layer, base, state, top, low)

    def advance(number, layer):
        section = lax.rem(number, SECTIONS)
        state, change = rates(number, layer)
        keep = jnp.where(section == 0, 0.0, jnp.where(section == 1, 0.75, 1.0 / 3.0)).astype(F32)
        take = jnp.where(section == 0, 1.0, jnp.where(section == 1, 0.25, 2.0 / 3.0)).astype(F32)
        for f in range(half):
            at = half * layer + f
            work[1 - lax.rem(number, 2), at] = keep * anchor[at] + take * (state[f] + TIME_STEP * change[f])

        @pl.when(section == SECTIONS - 1)
        def _():
            for f in range(half):
                at = half * layer + f
                anchor[at] = work[1 - lax.rem(number, 2), at]

    most = max(LAG * (lines - 1) + RUN_LAG_END, LAG * max(lines - 2, 1) + RUN_LAG_MID)

    @pl.loop(0, most + chunks - half + 1)
    def _(t):
        c_pair = t - near_lag
        c_up = t - LAG * line
        c_dn = t - LAG * (lines - 1 - line)
        c_fin = t - far_lag
        c_run = c_fin - run_lag

        @pl.when((c_pair >= 0) & (c_pair < parts))
        def _():
            await_bytes(cand.at[:, c_pair], r_cand.at[c_pair])

        @pl.when(inside(c_up))
        def _():
            @pl.when(dn_ok)
            def _():
                go_up(c_up).wait_recv()

            @pl.when(up_ok)
            def _():
                here = lax.div(owner_of(c_up), 2) == line
                out_up[c_up] = jnp.where(here, candidate(c_up), in_up[c_up])
                go_up(c_up).start()

        @pl.when(inside(c_dn))
        def _():
            @pl.when(up_ok)
            def _():
                go_dn(c_dn).wait_recv()

            @pl.when(dn_ok)
            def _():
                here = lax.div(owner_of(c_dn), 2) == line
                out_dn[c_dn] = jnp.where(here, candidate(c_dn), in_dn[c_dn])
                go_dn(c_dn).start()

        @pl.when(inside(c_fin))
        def _():
            at = lax.div(owner_of(c_fin), 2)
            q, f = lax.div(c_fin, half), half * core + lax.rem(c_fin, half)
            main[q, f, inner] = jnp.where(
                at == line, candidate(c_fin), jnp.where(at < line, in_up[c_fin], in_dn[c_fin])
            )
            spot = main.at[q, f, inner]
            remote(spot, spot, s_give, r_sec.at[q], sibling).start()

            @pl.when(lax.rem(c_fin, half) == half - 1)
            def _():
                for c in range(2):
                    for target, src, dst in (
                        (first_block, rows, 0), (last_block, HALO, HALO + rows)
                    ):
                        remote(
                            main.at[q, own_layer, pl.ds(src, HALO)],
                            main.at[q, own_layer, pl.ds(dst, HALO)],
                            s_edge, r_sec.at[q],
                            {"vec": target["vec"], "space": 2 * (target["space"] // 2) + c},
                        ).start()

        @pl.when(c_fin == half - 1)
        def _():
            await_bytes(anchor.at[:, inner], r_pert)
            for target, src, dst in ((first_block, rows, 0), (last_block, HALO, HALO + rows)):
                remote(
                    anchor.at[:, pl.ds(src, HALO)], anchor.at[:, pl.ds(dst, HALO)], s_side, r_side, target
                ).start()

        @pl.when(c_run == half - 1)
        def _():
            await_bytes(anchor.at[:, pl.ds(0, 2 * HALO)], r_side)
            await_bytes(anchor.at[:, pl.ds(0, 2 * HALO)], s_side)
            work[0] = anchor[...]

        @pl.when((c_run >= half - 1) & (c_run < chunks - 1) & (lax.rem(c_run, half) == half - 1))
        def _():
            number = lax.div(c_run, half)
            await_bytes(fresh, r_sec.at[number])
            advance(number, 0)

        @pl.when((c_run >= half) & (c_run < chunks) & (lax.rem(c_run, half) == 0))
        def _():
            advance(lax.div(c_run, half) - 1, 1)

    size_f, size_l = slice_shape(n, fields, cols)
    across = cols // (128 * size_l)
    slots = (fields // size_f) * across
    mine = 2 * line + core
    packed = n * n <= 128 and n % 8 == 0 and n * ns <= 64

    def slot(v):
        return n - 1 - v if packed else v

    def window(ref, j):
        f = pl.multiple_of(lax.div(j, across) * size_f, size_f)
        l = pl.multiple_of(lax.rem(j, across) * (128 * size_l), 128 * size_l)
        return ref.at[pl.ds(f, size_f), :, pl.ds(l, 128 * size_l)]

    def spread(d):
        to = lax.rem(mine + d, n)
        return to, {"vec": 2 * (to // 2) + side, "space": 2 * place + lax.rem(to, 2)}

    order = [d for d in sorted(range(n), key=lambda d: -min(d, n - d))]
    final = STEPS * SECTIONS - 1
    await_bytes(fresh, r_sec.at[final])
    mid = slice(HALO, HALO + rows)
    for layer in range(2):
        state, change = rates(final, layer)
        for f in range(half):
            at = half * layer + f
            x_ref[at] = anchor[at, mid] * (1.0 / 3.0) + (2.0 / 3.0) * (state[f][mid] + TIME_STEP * change[f][mid])
        if half % size_f and layer == 0:
            continue
        for d in order:
            to, where = spread(d)
            mine_now = (to < slots) & (to // across * size_f // half == layer) if half % size_f == 0 else to < slots
            if d:

                @pl.when(mine_now)
                def _():
                    remote(window(x_ref, to), cols_ref.at[slot(vector)], s_vec, r_vec, where).start()

    @pl.when(mine < slots)
    def _():
        cols_ref[slot(vector)] = window(x_ref, mine)[...]

    @pl.when(stay)
    def _():
        await_bytes(pool.at[pl.ds(0, parts)], s_cand)

    @pl.when(away)
    def _():
        await_bytes(pool.at[pl.ds(0, 2 * parts)], s_cand)
        await_bytes(anchor.at[:, inner], s_pert)

    await_bytes(out_up, s_give)
    await_bytes(rims, s_edge)

    @pl.when(up_ok)
    def _():
        await_bytes(out_up, s_up)

    @pl.when(dn_ok)
    def _():
        await_bytes(out_dn, s_dn)

    lanes = lax.broadcasted_iota(jnp.int32, (n, 128), 1)
    ranks = lax.broadcasted_iota(jnp.int32, (n, 128), 0)

    @pl.when(mine < slots)
    def _():
        await_bytes(cols_ref.at[pl.ds(0, n - 1)], r_vec)
        gram = jnp.zeros((n, 128), F32)
        for i in range(n):
            total = jnp.sum(cols_ref[...] * cols_ref[slot(i)][None], axis=(1, 2))
            if total.shape[-1] != 128:
                total = total.reshape(n, size_l, 128).sum(axis=1)
            gram = gram + jnp.where(lanes == i, jnp.sum(total, axis=1, keepdims=True), 0.0)
        mine_s[...] = gram

    @pl.when(mine >= slots)
    def _():
        mine_s[...] = jnp.zeros((n, 128), F32)

    if packed:
        row = jnp.sum(pltpu.roll(mine_s[...], 0, 1, stride=n, stride_axis=0), axis=0, keepdims=True)
        mine_v[...] = row
        rank = me * ns + tile
        reach = [(dv, ds) for dv in range(n) for ds in range(ns) if dv or ds]
        reach.sort(key=lambda e: -min(e[0], n - e[0]))
        for dv, ds in reach:
            where = {"vec": lax.rem(me + dv, n), "space": lax.rem(tile + ds, ns)}
            remote(mine_v, gvec.at[rank], s_gv, r_gv, where).start()
        gvec[rank] = row
        await_bytes(gvec.at[pl.ds(0, n * ns - 1)], r_gv)
        row = gvec[0]
        for i in range(1, n * ns):
            row = row + gvec[i]
        gram = pltpu.roll(jnp.broadcast_to(row, (n, 128)), 128 - n * (n - 1), 1, stride=n, stride_axis=0)
    else:
        for d in range(1, ns):
            to = lax.rem(tile + d, ns)
            remote(mine_s, gspace.at[tile], s_gs, r_gs, {"space": to}).start()
        gspace[tile] = mine_s[...]
        await_bytes(gspace.at[pl.ds(0, ns - 1)], r_gs)
        gram = gspace[0]
        for i in range(1, ns):
            gram = gram + gspace[i]
        mine_v[...] = gram
        for d in range(1, n):
            to = lax.rem(me + d, n)
            remote(mine_v, gvec.at[me], s_gv, r_gv, {"vec": to}).start()
        gvec[me] = gram
        await_bytes(gvec.at[pl.ds(0, n - 1)], r_gv)
        gram = gvec[0]
        for i in range(1, n):
            gram = gram + gvec[i]

    a = jnp.where(lanes < n, gram / entries, 0.0) + jnp.where(lanes == ranks + n, 1.0, 0.0)
    diagonal = jnp.ones((n, 1), F32)
    for k in range(n):
        column = a[:, k : k + 1]
        diagonal = jnp.where(ranks[:, :1] == k, column, diagonal)
        factor = jnp.where(ranks[:, :1] > k, column / column[k : k + 1, :], 0.0)
        a = a - factor * a[k : k + 1, :]
    a = a / jnp.sqrt(diagonal)
    upper_ref[...] = jnp.where(lanes >= ranks, a, 0.0)[:, :n]

    @pl.when(mine < slots)
    def _():
        for i in range(n):
            total = a[i : i + 1, n : n + 1][None] * cols_ref[slot(0)]
            for j in range(1, i + 1):
                total = total + a[i : i + 1, n + j : n + j + 1][None] * cols_ref[slot(j)]
            result[i] = total

        for d in range(n):
            i = lax.rem(vector + n // 2 + d, n)

            @pl.when((me != i) | away)
            def _():
                remote(
                    result.at[i], window(out_ref, mine), s_back, r_back, {"vec": i, "space": block}
                ).start()

        @pl.when(stay)
        def _():
            window(out_ref, mine)[...] = result[me]

    def drain(several, fewer, sem):
        @pl.when(fewer)
        def _():
            await_bytes(result.at[pl.ds(0, several - 1)], sem)

        @pl.when(jnp.logical_not(fewer))
        def _():
            await_bytes(result.at[pl.ds(0, several)], sem)

    drain(slots, stay & (mine < slots), r_back)
    drain(slots, mine < slots, s_vec)

    @pl.when(mine < slots)
    def _():
        drain(n, stay, s_back)

    if packed:
        await_bytes(gvec.at[pl.ds(0, n * ns - 1)], s_gv)
    else:
        await_bytes(gspace.at[pl.ds(0, ns - 1)], s_gs)
        await_bytes(gvec.at[pl.ds(0, n - 1)], s_gv)


def body(n, ns, perturbation, trajectory, step_order):
    pert, traj = perturbation[0], trajectory[0]
    fields, rows, cols = pert.shape
    sections = traj.shape[0]
    chunks, bf = STEPS * sections * (fields // 2), traj.dtype
    packed = n * n <= 128 and n % 8 == 0 and n * ns <= 64
    size_f, size_l = slice_shape(n, fields, cols)
    vmem = pl.BlockSpec(memory_space=pltpu.VMEM)
    hbm = pl.BlockSpec(memory_space=pl.ANY)
    piece = pltpu.VMEM((chunks, rows, cols), bf)
    full = pltpu.VMEM((fields, rows + 2 * HALO, cols), F32)
    slices = pltpu.VMEM((n, size_f, rows, 128 * size_l), F32)
    small = pltpu.VMEM((n, 128), F32)
    dma, one = pltpu.SemaphoreType.DMA, pltpu.SemaphoreType.DMA(())
    out, upper = pl.pallas_call(
        functools.partial(whole_kernel, n, ns, float(fields * rows * cols * ns)),
        out_shape=(pltpu.VMEM(pert.shape, F32), pltpu.VMEM((n, n), F32)),
        in_specs=[pl.BlockSpec(memory_space=pltpu.SMEM), hbm, hbm],
        out_specs=(vmem, vmem),
        scratch_shapes=[
            pltpu.VMEM((STEPS * sections, fields, rows + 2 * HALO, cols), bf),
            pltpu.VMEM((2, sections * (fields // 2), rows, cols), bf),
            piece, piece, piece, piece, piece,
            pltpu.VMEM((fields // 2, rows + 4 * HALO, cols), bf),
            pltpu.VMEM((STEPS * sections, fields, 2 * HALO, cols), bf),
            full, pltpu.VMEM((2, *full.shape), F32),
            pltpu.VMEM(pert.shape, F32), slices, slices,
            pltpu.VMEM((ns, n, 128), F32),
            pltpu.VMEM((n * ns, 1, 128) if packed else (n, n, 128), F32),
            small,
            pltpu.VMEM((1, 128), F32) if packed else small,
            dma((sections * (fields // 2),)), dma((chunks,)), dma((chunks,)), dma((STEPS * sections,)),
            one, one, one, one, one, one,
            one, one, one, one, one, one, one, one, one, one, one,
        ],
        compiler_params=pltpu.CompilerParams(collective_id=0, has_side_effects=True),
        name="whole",
    )(step_order, traj, pert)

    def finish(back_ref, upper_ref, out_ref, factor_ref, sems):
        copies = [
            pltpu.make_async_copy(back_ref, out_ref, sems.at[0]),
            pltpu.make_async_copy(upper_ref, factor_ref, sems.at[1]),
        ]
        for copy in copies:
            copy.start()
        for copy in copies:
            copy.wait()

    out, factor = pl.pallas_call(
        finish,
        out_shape=(jax.ShapeDtypeStruct(pert.shape, F32), jax.ShapeDtypeStruct((n, n), F32)),
        in_specs=[vmem, vmem],
        out_specs=(hbm, hbm),
        scratch_shapes=[dma((2,))],
        name="finish",
    )(
        pltpu.with_memory_space_constraint(out, pltpu.VMEM),
        pltpu.with_memory_space_constraint(upper, pltpu.VMEM),
    )
    return out[None], factor


def solution(mesh):
    n, ns = mesh.shape["vec"], mesh.shape["space"]
    in_specs = (P("vec", None, "space", None), P("vec", None, None, "space", None), P())
    out_specs = (P("vec", None, "space", None), P())
    return jax.shard_map(
        functools.partial(body, n, ns), mesh=mesh, in_specs=in_specs, out_specs=out_specs, check_vma=False
    )
```

```python
import functools

import jax
import jax.numpy as jnp
from jax import lax
from jax.experimental import pallas as pl
from jax.experimental.pallas import tpu as pltpu
from jax.sharding import PartitionSpec as P

STEPS = 2
SECTIONS = 3
LAG = 6
RUN_LAG_END = 8
RUN_LAG_MID = 15
HALO = 8

GRAVITY_TOP = 1.0
GRAVITY_LOW = 0.5
DEPTH_TOP = 1.0
DEPTH_LOW = 1.0
CORIOLIS = 0.3
TIME_STEP = 0.25

MESH = pl.DeviceIdType.MESH
F32 = jnp.float32


def remote(src, dst, send, recv, target):
    return pltpu.make_async_remote_copy(
        src_ref=src, dst_ref=dst, send_sem=send, recv_sem=recv, device_id=target, device_id_type=MESH
    )


def await_bytes(ref, sem):
    pltpu.make_async_copy(ref, ref, sem).wait()


def twice_dx(field):
    count = field.shape[0]
    return pltpu.roll(field, count - 1, 0) - pltpu.roll(field, 1, 0)


def twice_dy(field):
    count = field.shape[1]
    return pltpu.roll(field, count - 1, 1) - pltpu.roll(field, 1, 1)


def tangent(layer, base, state, top, low):
    pressure = GRAVITY_TOP * (top + low)
    if layer:
        pressure = pressure + GRAVITY_LOW * low
    depth = base[0] + (DEPTH_TOP, DEPTH_LOW)[layer]
    u, v = base[1], base[2]
    dh, du, dv = state
    return [
        twice_dx(depth * du + dh * u) + twice_dy(depth * dv + dh * v),
        (u * twice_dx(du) + du * twice_dx(u)) + (v * twice_dy(du) + dv * twice_dy(u))
        + twice_dx(pressure) - (2 * CORIOLIS) * dv,
        (u * twice_dx(dv) + du * twice_dx(v)) + (v * twice_dy(dv) + dv * twice_dy(v))
        + twice_dy(pressure) + (2 * CORIOLIS) * du,
    ]


def slice_shape(n, fields, cols):
    lanes = cols // 128
    best = None
    for f in range(1, fields + 1):
        for l in range(1, lanes + 1):
            if fields % f or lanes % l or (fields // f) * (lanes // l) > n:
                continue
            if best is None or f * l < best[0] * best[1]:
                best = (f, l)
    return best


def paired(value, mask, count):
    if count & (count - 1):
        return lax.rem(value + mask, count)
    made, bit = 0, 1
    while bit < count:
        digit = lax.rem(lax.div(value, bit), 2)
        made = made + bit * (1 - digit if mask & bit else digit)
        bit *= 2
    return made


def far_first(count):
    return sorted(range(count), key=lambda m: (-m.bit_length(), m))


def whole_kernel(
    n, ns, entries, order_ref, traj_ref, pert_ref,
    out_ref, upper_ref,
    main, cand, in_up, in_dn, out_up, out_dn, pool, fresh, rims, anchor, work,
    x_ref, cols_ref, result, gspace, gvec, mine_s, mine_v,
    r_cand, r_up, r_dn, r_sec, r_pert, r_side, r_vec, r_gs, r_gv, r_back,
    s_cand, s_pert, s_side, s_up, s_dn, s_give, s_edge, s_vec, s_gs, s_gv, s_back,
):
    me = lax.axis_index("vec")
    tile = lax.axis_index("space")
    fields, rows, cols = pert_ref.shape
    half = fields // 2
    chunks = STEPS * SECTIONS * half
    parts = SECTIONS * half
    lines, places = n // 2, ns // 2
    side, line = lax.rem(me, 2), me // 2
    core, place = lax.rem(tile, 2), tile // 2
    flip = lax.rem(place, 2)

    def differs(a, b):
        return a + b - 2 * a * b

    home = differs(side, flip)
    stay = core == home
    away = core != home
    block = 2 * place + home
    vector = 2 * line + differs(core, flip)
    sibling = {"space": 2 * place + 1 - core}
    up_ok = line < lines - 1
    dn_ok = line > 0

    def worker(v, t):
        p = t // 2
        turn = lax.rem(p, 2)
        return {
            "vec": 2 * (v // 2) + differs(lax.rem(t, 2), turn),
            "space": 2 * p + differs(lax.rem(v, 2), turn),
        }

    barrier = pltpu.get_barrier_semaphore()
    near = sorted({0, 1 % places, places - 1})
    count = 0
    for across in range(2):
        for step in near:
            for c in range(2):
                if (across == 0 and step == 0 and c == 0) or (across and step):
                    continue
                where = {
                    "vec": me + across * (1 - 2 * side),
                    "space": 2 * lax.rem(place + step, places) + lax.rem(core + c, 2),
                }
                pl.semaphore_signal(barrier, inc=1, device_id=where, device_id_type=MESH)
                count += 1

    @pl.when(up_ok)
    def _():
        pl.semaphore_signal(barrier, inc=1, device_id={"vec": me + 2}, device_id_type=MESH)

    @pl.when(dn_ok)
    def _():
        pl.semaphore_signal(barrier, inc=1, device_id={"vec": me - 2}, device_id_type=MESH)

    inner = pl.ds(HALO, rows)

    @pl.when(stay)
    def _():
        @pl.loop(0, parts)
        def _(p):
            k, f = lax.div(p, half), lax.rem(p, half)
            pltpu.make_async_copy(traj_ref.at[k, half * core + f], cand.at[0, p], r_cand.at[p]).start()

        pltpu.make_async_copy(pert_ref, anchor.at[:, inner], r_pert).start()

    pl.semaphore_wait(barrier, count + up_ok.astype(jnp.int32) + dn_ok.astype(jnp.int32))

    other = me + 1 - 2 * side

    @pl.when(stay)
    def _():
        @pl.loop(0, parts)
        def _(p):
            k, f = lax.div(p, half), lax.rem(p, half)
            remote(
                traj_ref.at[k, half * (1 - core) + f], cand.at[0, p], s_cand, r_cand.at[p], sibling
            ).start()

    @pl.when(away)
    def _():
        @pl.loop(0, parts)
        def _(p):
            k, f = lax.div(p, half), lax.rem(p, half)
            for c in range(2):
                remote(
                    traj_ref.at[k, half * c + f], cand.at[1, p], s_cand, r_cand.at[p],
                    {"vec": other, "space": 2 * place + c},
                ).start()

    @pl.when(away)
    def _():
        remote(
            pert_ref, anchor.at[:, inner], s_pert, r_pert,
            {"vec": other, "space": 2 * place + 1 - core},
        ).start()

    def go_up(c):
        return remote(out_up.at[c], in_up.at[c], s_up, r_up.at[c], {"vec": me + 2})

    def go_dn(c):
        return remote(out_dn.at[c], in_dn.at[c], s_dn, r_dn.at[c], {"vec": me - 2})

    def owner_of(c):
        return jnp.where(c >= parts, order_ref[1], order_ref[0])

    def candidate(c):
        p = lax.rem(c, parts)
        return jnp.where(owner_of(c) == me, cand[0, p], cand[1, p])

    def inside(c):
        return (c >= 0) & (c < chunks)

    first_block = worker(vector, lax.rem(block + 1, ns))
    last_block = worker(vector, lax.rem(block + ns - 1, ns))
    own_layer = pl.ds(half * core, half)

    run_lag = jnp.where(up_ok & dn_ok, RUN_LAG_MID, RUN_LAG_END)
    near_lag = LAG * jnp.minimum(line, lines - 1 - line)
    far_lag = LAG * jnp.maximum(line, lines - 1 - line)

    def rates(number, layer):
        now = lax.rem(number, 2)
        at = half * layer
        base = [main[number, at + f].astype(F32) for f in range(half)]
        state = [work[now, at + f] for f in range(half)]
        top = state[0] if layer == 0 else work[now, 0]
        low = state[0] if layer == 1 else work[now, half]
        return state, tangent(layer, base, state, top, low)

    def advance(number, layer):
        section = lax.rem(number, SECTIONS)
        state, change = rates(number, layer)
        keep = jnp.where(section == 0, 0.0, jnp.where(section == 1, 0.75, 1.0 / 3.0)).astype(F32)
        take = jnp.where(section == 0, 1.0, jnp.where(section == 1, 0.25, 2.0 / 3.0)).astype(F32)
        for f in range(half):
            at = half * layer + f
            work[1 - lax.rem(number, 2), at] = keep * anchor[at] + take * (state[f] - (0.5 * TIME_STEP) * change[f])

        @pl.when(section == SECTIONS - 1)
        def _():
            for f in range(half):
                at = half * layer + f
                anchor[at] = work[1 - lax.rem(number, 2), at]

    most = max(LAG * (lines - 1) + RUN_LAG_END, LAG * max(lines - 2, 1) + RUN_LAG_MID)

    @pl.loop(0, most + chunks - half + 1)
    def _(t):
        c_pair = t - near_lag
        c_up = t - LAG * line
        c_dn = t - LAG * (lines - 1 - line)
        c_fin = t - far_lag
        c_run = c_fin - run_lag

        @pl.when((c_pair >= 0) & (c_pair < parts))
        def _():
            await_bytes(cand.at[:, c_pair], r_cand.at[c_pair])

        @pl.when(inside(c_up))
        def _():
            @pl.when(dn_ok)
            def _():
                go_up(c_up).wait_recv()

            @pl.when(up_ok)
            def _():
                here = lax.div(owner_of(c_up), 2) == line
                out_up[c_up] = jnp.where(here, candidate(c_up), in_up[c_up])
                go_up(c_up).start()

        @pl.when(inside(c_dn))
        def _():
            @pl.when(up_ok)
            def _():
                go_dn(c_dn).wait_recv()

            @pl.when(dn_ok)
            def _():
                here = lax.div(owner_of(c_dn), 2) == line
                out_dn[c_dn] = jnp.where(here, candidate(c_dn), in_dn[c_dn])
                go_dn(c_dn).start()

        @pl.when(inside(c_fin))
        def _():
            at = lax.div(owner_of(c_fin), 2)
            q, f = lax.div(c_fin, half), half * core + lax.rem(c_fin, half)
            main[q, f, inner] = jnp.where(
                at == line, candidate(c_fin), jnp.where(at < line, in_up[c_fin], in_dn[c_fin])
            )
            spot = main.at[q, f, inner]
            remote(spot, spot, s_give, r_sec.at[q], sibling).start()

            @pl.when(lax.rem(c_fin, half) == half - 1)
            def _():
                for c in range(2):
                    for target, src, dst in (
                        (first_block, rows, 0), (last_block, HALO, HALO + rows)
                    ):
                        remote(
                            main.at[q, own_layer, pl.ds(src, HALO)],
                            main.at[q, own_layer, pl.ds(dst, HALO)],
                            s_edge, r_sec.at[q],
                            {"vec": target["vec"], "space": 2 * (target["space"] // 2) + c},
                        ).start()

        @pl.when(c_fin == half - 1)
        def _():
            await_bytes(anchor.at[:, inner], r_pert)
            for target, src, dst in ((first_block, rows, 0), (last_block, HALO, HALO + rows)):
                remote(
                    anchor.at[:, pl.ds(src, HALO)], anchor.at[:, pl.ds(dst, HALO)], s_side, r_side, target
                ).start()

        @pl.when(c_run == half - 1)
        def _():
            await_bytes(anchor.at[:, pl.ds(0, 2 * HALO)], r_side)
            await_bytes(anchor.at[:, pl.ds(0, 2 * HALO)], s_side)
            work[0] = anchor[...]

        @pl.when((c_run >= half - 1) & (c_run < chunks - 1) & (lax.rem(c_run, half) == half - 1))
        def _():
            number = lax.div(c_run, half)
            await_bytes(fresh, r_sec.at[number])
            advance(number, 0)

        @pl.when((c_run >= half) & (c_run < chunks) & (lax.rem(c_run, half) == 0))
        def _():
            advance(lax.div(c_run, half) - 1, 1)

    size_f, size_l = slice_shape(n, fields, cols)
    across = cols // (128 * size_l)
    slots = (fields // size_f) * across
    mine = 2 * line + core
    packed = n * n <= 128 and n % 8 == 0 and n * ns <= 64

    def slot(v):
        return n - 1 - v if packed else v

    def window(ref, j):
        f = pl.multiple_of(lax.div(j, across) * size_f, size_f)
        l = pl.multiple_of(lax.rem(j, across) * (128 * size_l), 128 * size_l)
        return ref.at[pl.ds(f, size_f), :, pl.ds(l, 128 * size_l)]

    def spread(d):
        to = paired(mine, d, n)
        return to, {"vec": 2 * (to // 2) + side, "space": 2 * place + lax.rem(to, 2)}

    order = [2 * m + c for m in far_first(lines) for c in range(2)]
    final = STEPS * SECTIONS - 1
    await_bytes(fresh, r_sec.at[final])
    mid = slice(HALO, HALO + rows)
    for layer in range(2):
        state, change = rates(final, layer)
        for f in range(half):
            at = half * layer + f
            x_ref[at] = anchor[at, mid] * (1.0 / 3.0) + (2.0 / 3.0) * (state[f][mid] - (0.5 * TIME_STEP) * change[f][mid])
        if half % size_f and layer == 0:
            continue
        for d in order:
            to, where = spread(d)
            mine_now = (to < slots) & (to // across * size_f // half == layer) if half % size_f == 0 else to < slots
            if d:

                @pl.when(mine_now)
                def _():
                    remote(window(x_ref, to), cols_ref.at[slot(vector)], s_vec, r_vec, where).start()

    @pl.when(mine < slots)
    def _():
        cols_ref[slot(vector)] = window(x_ref, mine)[...]

    @pl.when(stay)
    def _():
        await_bytes(pool.at[pl.ds(0, parts)], s_cand)

    @pl.when(away)
    def _():
        await_bytes(pool.at[pl.ds(0, 2 * parts)], s_cand)
        await_bytes(anchor.at[:, inner], s_pert)

    await_bytes(out_up, s_give)
    await_bytes(rims, s_edge)

    @pl.when(up_ok)
    def _():
        await_bytes(out_up, s_up)

    @pl.when(dn_ok)
    def _():
        await_bytes(out_dn, s_dn)

    lanes = lax.broadcasted_iota(jnp.int32, (n, 128), 1)
    ranks = lax.broadcasted_iota(jnp.int32, (n, 128), 0)

    @pl.when(mine < slots)
    def _():
        await_bytes(cols_ref.at[pl.ds(0, n - 1)], r_vec)
        gram = jnp.zeros((n, 128), F32)
        for i in range(n):
            total = jnp.sum(cols_ref[...] * cols_ref[slot(i)][None], axis=(1, 2))
            if total.shape[-1] != 128:
                total = total.reshape(n, size_l, 128).sum(axis=1)
            gram = gram + jnp.where(lanes == i, jnp.sum(total, axis=1, keepdims=True), 0.0)
        mine_s[...] = gram

    @pl.when(mine >= slots)
    def _():
        mine_s[...] = jnp.zeros((n, 128), F32)

    if packed:
        row = jnp.sum(pltpu.roll(mine_s[...], 0, 1, stride=n, stride_axis=0), axis=0, keepdims=True)
        mine_v[...] = row
        rank = me * ns + tile
        reach = [(2 * m + c, ds) for m in far_first(lines) for c in range(2) for ds in range(ns) if m or c or ds]
        for dv, ds in reach:
            where = {"vec": paired(me, dv, n), "space": paired(tile, ds, ns)}
            remote(mine_v, gvec.at[rank], s_gv, r_gv, where).start()
        gvec[rank] = row
        await_bytes(gvec.at[pl.ds(0, n * ns - 1)], r_gv)
        row = gvec[0]
        for i in range(1, n * ns):
            row = row + gvec[i]
        gram = pltpu.roll(jnp.broadcast_to(row, (n, 128)), 128 - n * (n - 1), 1, stride=n, stride_axis=0)
    else:
        for d in range(1, ns):
            to = lax.rem(tile + d, ns)
            remote(mine_s, gspace.at[tile], s_gs, r_gs, {"space": to}).start()
        gspace[tile] = mine_s[...]
        await_bytes(gspace.at[pl.ds(0, ns - 1)], r_gs)
        gram = gspace[0]
        for i in range(1, ns):
            gram = gram + gspace[i]
        mine_v[...] = gram
        for d in range(1, n):
            to = lax.rem(me + d, n)
            remote(mine_v, gvec.at[me], s_gv, r_gv, {"vec": to}).start()
        gvec[me] = gram
        await_bytes(gvec.at[pl.ds(0, n - 1)], r_gv)
        gram = gvec[0]
        for i in range(1, n):
            gram = gram + gvec[i]

    a = jnp.where(lanes < n, gram / entries, 0.0) + jnp.where(lanes == ranks + n, 1.0, 0.0)
    diagonal = jnp.ones((n, 1), F32)
    for k in range(n):
        column = a[:, k : k + 1]
        diagonal = jnp.where(ranks[:, :1] == k, column, diagonal)
        factor = jnp.where(ranks[:, :1] > k, column / column[k : k + 1, :], 0.0)
        a = a - factor * a[k : k + 1, :]
    a = a / jnp.sqrt(diagonal)
    upper_ref[...] = jnp.where(lanes >= ranks, a, 0.0)[:, :n]

    @pl.when(mine < slots)
    def _():
        for i in range(n):
            total = a[i : i + 1, n : n + 1][None] * cols_ref[slot(0)]
            for j in range(1, i + 1):
                total = total + a[i : i + 1, n + j : n + j + 1][None] * cols_ref[slot(j)]
            result[i] = total

        for d in order:
            i = paired(vector, d, n)

            @pl.when((me != i) | away)
            def _():
                remote(
                    result.at[i], window(out_ref, mine), s_back, r_back, {"vec": i, "space": block}
                ).start()

        @pl.when(stay)
        def _():
            window(out_ref, mine)[...] = result[me]

    def drain(several, fewer, sem):
        @pl.when(fewer)
        def _():
            await_bytes(result.at[pl.ds(0, several - 1)], sem)

        @pl.when(jnp.logical_not(fewer))
        def _():
            await_bytes(result.at[pl.ds(0, several)], sem)

    drain(slots, stay & (mine < slots), r_back)
    drain(slots, mine < slots, s_vec)

    @pl.when(mine < slots)
    def _():
        drain(n, stay, s_back)

    if packed:
        await_bytes(gvec.at[pl.ds(0, n * ns - 1)], s_gv)
    else:
        await_bytes(gspace.at[pl.ds(0, ns - 1)], s_gs)
        await_bytes(gvec.at[pl.ds(0, n - 1)], s_gv)


def body(n, ns, perturbation, trajectory, step_order):
    pert, traj = perturbation[0], trajectory[0]
    fields, rows, cols = pert.shape
    sections = traj.shape[0]
    chunks, bf = STEPS * sections * (fields // 2), traj.dtype
    packed = n * n <= 128 and n % 8 == 0 and n * ns <= 64
    size_f, size_l = slice_shape(n, fields, cols)
    vmem = pl.BlockSpec(memory_space=pltpu.VMEM)
    hbm = pl.BlockSpec(memory_space=pl.ANY)
    piece = pltpu.VMEM((chunks, rows, cols), bf)
    full = pltpu.VMEM((fields, rows + 2 * HALO, cols), F32)
    slices = pltpu.VMEM((n, size_f, rows, 128 * size_l), F32)
    small = pltpu.VMEM((n, 128), F32)
    dma, one = pltpu.SemaphoreType.DMA, pltpu.SemaphoreType.DMA(())
    out, upper = pl.pallas_call(
        functools.partial(whole_kernel, n, ns, float(fields * rows * cols * ns)),
        out_shape=(pltpu.VMEM(pert.shape, F32), pltpu.VMEM((n, n), F32)),
        in_specs=[pl.BlockSpec(memory_space=pltpu.SMEM), hbm, hbm],
        out_specs=(vmem, vmem),
        scratch_shapes=[
            pltpu.VMEM((STEPS * sections, fields, rows + 2 * HALO, cols), bf),
            pltpu.VMEM((2, sections * (fields // 2), rows, cols), bf),
            piece, piece, piece, piece, piece,
            pltpu.VMEM((fields // 2, rows + 4 * HALO, cols), bf),
            pltpu.VMEM((STEPS * sections, fields, 2 * HALO, cols), bf),
            full, pltpu.VMEM((2, *full.shape), F32),
            pltpu.VMEM(pert.shape, F32), slices, slices,
            pltpu.VMEM((ns, n, 128), F32),
            pltpu.VMEM((n * ns, 1, 128) if packed else (n, n, 128), F32),
            small,
            pltpu.VMEM((1, 128), F32) if packed else small,
            dma((sections * (fields // 2),)), dma((chunks,)), dma((chunks,)), dma((STEPS * sections,)),
            one, one, one, one, one, one,
            one, one, one, one, one, one, one, one, one, one, one,
        ],
        compiler_params=pltpu.CompilerParams(collective_id=0, has_side_effects=True),
        name="whole",
    )(step_order, traj, pert)

    def finish(back_ref, upper_ref, out_ref, factor_ref, sems):
        copies = [
            pltpu.make_async_copy(back_ref, out_ref, sems.at[0]),
            pltpu.make_async_copy(upper_ref, factor_ref, sems.at[1]),
        ]
        for copy in copies:
            copy.start()
        for copy in copies:
            copy.wait()

    out, factor = pl.pallas_call(
        finish,
        out_shape=(jax.ShapeDtypeStruct(pert.shape, F32), jax.ShapeDtypeStruct((n, n), F32)),
        in_specs=[vmem, vmem],
        out_specs=(hbm, hbm),
        scratch_shapes=[dma((2,))],
        name="finish",
    )(
        pltpu.with_memory_space_constraint(out, pltpu.VMEM),
        pltpu.with_memory_space_constraint(upper, pltpu.VMEM),
    )
    return out[None], factor


def solution(mesh):
    n, ns = mesh.shape["vec"], mesh.shape["space"]
    in_specs = (P("vec", None, "space", None), P("vec", None, None, "space", None), P())
    out_specs = (P("vec", None, "space", None), P())
    return jax.shard_map(
        functools.partial(body, n, ns), mesh=mesh, in_specs=in_specs, out_specs=out_specs, check_vma=False
    )
```

```python
import functools

import jax
import jax.numpy as jnp
from jax import lax
from jax.experimental import pallas as pl
from jax.experimental.pallas import tpu as pltpu
from jax.sharding import PartitionSpec as P

STEPS = 2
SECTIONS = 3
LAG_UP = 6
LAG_DN = 6
RUN_LAG_END = 8
RUN_LAG_MID = 15
HALO = 8

GRAVITY_TOP = 1.0
GRAVITY_LOW = 0.5
DEPTH_TOP = 1.0
DEPTH_LOW = 1.0
CORIOLIS = 0.3
TIME_STEP = 0.25

MESH = pl.DeviceIdType.MESH
F32 = jnp.float32


def remote(src, dst, send, recv, target):
    return pltpu.make_async_remote_copy(
        src_ref=src, dst_ref=dst, send_sem=send, recv_sem=recv, device_id=target, device_id_type=MESH
    )


def await_bytes(ref, sem):
    pltpu.make_async_copy(ref, ref, sem).wait()


def twice_dx(field):
    count = field.shape[0]
    return pltpu.roll(field, count - 1, 0) - pltpu.roll(field, 1, 0)


def twice_dy(field):
    count = field.shape[1]
    return pltpu.roll(field, count - 1, 1) - pltpu.roll(field, 1, 1)


def tangent(layer, base, state, top, low):
    pressure = GRAVITY_TOP * (top + low)
    if layer:
        pressure = pressure + GRAVITY_LOW * low
    depth = base[0] + (DEPTH_TOP, DEPTH_LOW)[layer]
    u, v = base[1], base[2]
    dh, du, dv = state
    return [
        twice_dx(depth * du + dh * u) + twice_dy(depth * dv + dh * v),
        (u * twice_dx(du) + du * twice_dx(u)) + (v * twice_dy(du) + dv * twice_dy(u))
        + twice_dx(pressure) - (2 * CORIOLIS) * dv,
        (u * twice_dx(dv) + du * twice_dx(v)) + (v * twice_dy(dv) + dv * twice_dy(v))
        + twice_dy(pressure) + (2 * CORIOLIS) * du,
    ]


def slice_shape(n, fields, cols):
    lanes = cols // 128
    best = None
    for f in range(1, fields + 1):
        for l in range(1, lanes + 1):
            if fields % f or lanes % l or (fields // f) * (lanes // l) > n:
                continue
            if best is None or f * l < best[0] * best[1]:
                best = (f, l)
    return best


def paired(value, mask, count):
    if count & (count - 1):
        return lax.rem(value + mask, count)
    made, bit = 0, 1
    while bit < count:
        digit = lax.rem(lax.div(value, bit), 2)
        made = made + bit * (1 - digit if mask & bit else digit)
        bit *= 2
    return made


def far_first(count):
    return sorted(range(count), key=lambda m: (-m.bit_length(), m))


def whole_kernel(
    n, ns, entries, order_in, traj_ref, pert_ref,
    out_ref, upper_ref,
    order_ref, main, cand, in_up, in_dn, out_up, out_dn, pool, fresh, rims, anchor, work,
    x_ref, cols_ref, result, gspace, gvec, mine_s, mine_v,
    r_order, r_cand, r_up, r_dn, r_sec, r_pert, r_side, r_vec, r_gs, r_gv, r_back,
    s_cand, s_pert, s_side, s_up, s_dn, s_give, s_edge, s_vec, s_gs, s_gv, s_back,
):
    me = lax.axis_index("vec")
    tile = lax.axis_index("space")
    fields, rows, cols = pert_ref.shape
    half = fields // 2
    chunks = STEPS * SECTIONS * half
    parts = SECTIONS * half
    lines, places = n // 2, ns // 2
    side, line = lax.rem(me, 2), me // 2
    core, place = lax.rem(tile, 2), tile // 2
    flip = lax.rem(place, 2)

    def differs(a, b):
        return a + b - 2 * a * b

    home = differs(side, flip)
    stay = core == home
    away = core != home
    block = 2 * place + home
    vector = 2 * line + differs(core, flip)
    sibling = {"space": 2 * place + 1 - core}
    up_ok = line < lines - 1
    dn_ok = line > 0

    def worker(v, t):
        p = t // 2
        turn = lax.rem(p, 2)
        return {
            "vec": 2 * (v // 2) + differs(lax.rem(t, 2), turn),
            "space": 2 * p + differs(lax.rem(v, 2), turn),
        }

    barrier = pltpu.get_barrier_semaphore()
    near = sorted({0, 1 % places, places - 1})
    count = 0
    for across in range(2):
        for step in near:
            for c in range(2):
                if (across == 0 and step == 0 and c == 0) or (across and step):
                    continue
                where = {
                    "vec": me + across * (1 - 2 * side),
                    "space": 2 * lax.rem(place + step, places) + lax.rem(core + c, 2),
                }
                pl.semaphore_signal(barrier, inc=1, device_id=where, device_id_type=MESH)
                count += 1

    @pl.when(up_ok)
    def _():
        pl.semaphore_signal(barrier, inc=1, device_id={"vec": me + 2}, device_id_type=MESH)

    @pl.when(dn_ok)
    def _():
        pl.semaphore_signal(barrier, inc=1, device_id={"vec": me - 2}, device_id_type=MESH)

    inner = pl.ds(HALO, rows)
    order_copy = pltpu.make_async_copy(order_in, order_ref, r_order)
    order_copy.start()

    @pl.when(stay)
    def _():
        @pl.loop(0, parts)
        def _(p):
            k, f = lax.div(p, half), lax.rem(p, half)
            pltpu.make_async_copy(traj_ref.at[k, half * core + f], cand.at[0, p], r_cand.at[p]).start()

        pltpu.make_async_copy(pert_ref, anchor.at[:, inner], r_pert).start()

    pl.semaphore_wait(barrier, count + up_ok.astype(jnp.int32) + dn_ok.astype(jnp.int32))

    other = me + 1 - 2 * side

    @pl.when(stay)
    def _():
        @pl.loop(0, parts)
        def _(p):
            k, f = lax.div(p, half), lax.rem(p, half)
            remote(
                traj_ref.at[k, half * (1 - core) + f], cand.at[0, p], s_cand, r_cand.at[p], sibling
            ).start()

    @pl.when(away)
    def _():
        @pl.loop(0, parts)
        def _(p):
            k, f = lax.div(p, half), lax.rem(p, half)
            for c in range(2):
                remote(
                    traj_ref.at[k, half * c + f], cand.at[1, p], s_cand, r_cand.at[p],
                    {"vec": other, "space": 2 * place + c},
                ).start()

    @pl.when(away)
    def _():
        remote(
            pert_ref, anchor.at[:, inner], s_pert, r_pert,
            {"vec": other, "space": 2 * place + 1 - core},
        ).start()

    def go_up(c):
        return remote(out_up.at[c], in_up.at[c], s_up, r_up.at[c], {"vec": me + 2})

    def go_dn(c):
        return remote(out_dn.at[c], in_dn.at[c], s_dn, r_dn.at[c], {"vec": me - 2})

    def owner_of(c):
        return jnp.where(c >= parts, order_ref[1], order_ref[0])

    def candidate(c):
        p = lax.rem(c, parts)
        return jnp.where(owner_of(c) == me, cand[0, p], cand[1, p])

    def inside(c):
        return (c >= 0) & (c < chunks)

    first_block = worker(vector, lax.rem(block + 1, ns))
    last_block = worker(vector, lax.rem(block + ns - 1, ns))
    own_layer = pl.ds(half * core, half)

    run_lag = jnp.where(up_ok & dn_ok, RUN_LAG_MID, RUN_LAG_END)
    up_lag = LAG_UP * line
    dn_lag = LAG_DN * (lines - 1 - line)
    near_lag = jnp.where(up_ok & dn_ok, jnp.minimum(up_lag, dn_lag), 0)
    far_lag = jnp.maximum(up_lag, dn_lag)
    most = max(
        max(LAG_UP * l, LAG_DN * (lines - 1 - l)) + (RUN_LAG_MID if 0 < l < lines - 1 else RUN_LAG_END)
        for l in range(lines)
    )

    def rates(number, layer):
        now = lax.rem(number, 2)
        at = half * layer
        base = [main[number, at + f].astype(F32) for f in range(half)]
        state = [work[now, at + f] for f in range(half)]
        top = state[0] if layer == 0 else work[now, 0]
        low = state[0] if layer == 1 else work[now, half]
        return state, tangent(layer, base, state, top, low)

    def advance(number, layer):
        section = lax.rem(number, SECTIONS)
        state, change = rates(number, layer)
        keep = jnp.where(section == 0, 0.0, jnp.where(section == 1, 0.75, 1.0 / 3.0)).astype(F32)
        take = jnp.where(section == 0, 1.0, jnp.where(section == 1, 0.25, 2.0 / 3.0)).astype(F32)
        for f in range(half):
            at = half * layer + f
            work[1 - lax.rem(number, 2), at] = keep * anchor[at] + take * (state[f] - (0.5 * TIME_STEP) * change[f])

        @pl.when(section == SECTIONS - 1)
        def _():
            for f in range(half):
                at = half * layer + f
                anchor[at] = work[1 - lax.rem(number, 2), at]

    order_copy.wait()

    @pl.loop(0, most + chunks - half + 1)
    def _(t):
        c_pair = t - near_lag
        c_up = t - up_lag
        c_dn = t - dn_lag
        c_fin = t - far_lag
        c_run = c_fin - run_lag

        @pl.when((c_pair >= 0) & (c_pair < parts))
        def _():
            await_bytes(cand.at[:, c_pair], r_cand.at[c_pair])

        @pl.when(inside(c_up))
        def _():
            @pl.when(dn_ok)
            def _():
                go_up(c_up).wait_recv()

            @pl.when(up_ok)
            def _():
                here = lax.div(owner_of(c_up), 2) == line
                out_up[c_up] = jnp.where(here, candidate(c_up), in_up[c_up])
                go_up(c_up).start()

        @pl.when(inside(c_dn))
        def _():
            @pl.when(up_ok)
            def _():
                go_dn(c_dn).wait_recv()

            @pl.when(dn_ok)
            def _():
                here = lax.div(owner_of(c_dn), 2) == line
                out_dn[c_dn] = jnp.where(here, candidate(c_dn), in_dn[c_dn])
                go_dn(c_dn).start()

        @pl.when(inside(c_fin))
        def _():
            at = lax.div(owner_of(c_fin), 2)
            q, f = lax.div(c_fin, half), half * core + lax.rem(c_fin, half)
            main[q, f, inner] = jnp.where(
                at == line, candidate(c_fin), jnp.where(at < line, in_up[c_fin], in_dn[c_fin])
            )
            spot = main.at[q, f, inner]
            remote(spot, spot, s_give, r_sec.at[q], sibling).start()

            @pl.when(lax.rem(c_fin, half) == half - 1)
            def _():
                for c in range(2):
                    for target, src, dst in (
                        (first_block, rows, 0), (last_block, HALO, HALO + rows)
                    ):
                        remote(
                            main.at[q, own_layer, pl.ds(src, HALO)],
                            main.at[q, own_layer, pl.ds(dst, HALO)],
                            s_edge, r_sec.at[q],
                            {"vec": target["vec"], "space": 2 * (target["space"] // 2) + c},
                        ).start()

        @pl.when(c_fin == half - 1)
        def _():
            await_bytes(anchor.at[:, inner], r_pert)
            for target, src, dst in ((first_block, rows, 0), (last_block, HALO, HALO + rows)):
                remote(
                    anchor.at[:, pl.ds(src, HALO)], anchor.at[:, pl.ds(dst, HALO)], s_side, r_side, target
                ).start()

        @pl.when(c_run == half - 1)
        def _():
            await_bytes(anchor.at[:, pl.ds(0, 2 * HALO)], r_side)
            await_bytes(anchor.at[:, pl.ds(0, 2 * HALO)], s_side)
            work[0] = anchor[...]

        @pl.when((c_run >= half - 1) & (c_run < chunks - 1) & (lax.rem(c_run, half) == half - 1))
        def _():
            number = lax.div(c_run, half)
            await_bytes(fresh, r_sec.at[number])
            advance(number, 0)

        @pl.when((c_run >= half) & (c_run < chunks) & (lax.rem(c_run, half) == 0))
        def _():
            advance(lax.div(c_run, half) - 1, 1)

    size_f, size_l = slice_shape(n, fields, cols)
    across = cols // (128 * size_l)
    slots = (fields // size_f) * across
    mine = 2 * line + core
    packed = n * n <= 128 and n % 8 == 0 and n * ns <= 64

    def slot(v):
        return n - 1 - v if packed else v

    def window(ref, j):
        f = pl.multiple_of(lax.div(j, across) * size_f, size_f)
        l = pl.multiple_of(lax.rem(j, across) * (128 * size_l), 128 * size_l)
        return ref.at[pl.ds(f, size_f), :, pl.ds(l, 128 * size_l)]

    def spread(d):
        to = paired(mine, d, n)
        return to, {"vec": 2 * (to // 2) + side, "space": 2 * place + lax.rem(to, 2)}

    order = [2 * m + c for m in far_first(lines) for c in range(2)]
    final = STEPS * SECTIONS - 1
    await_bytes(fresh, r_sec.at[final])
    mid = slice(HALO, HALO + rows)
    for layer in range(2):
        state, change = rates(final, layer)
        for f in range(half):
            at = half * layer + f
            x_ref[at] = anchor[at, mid] * (1.0 / 3.0) + (2.0 / 3.0) * (state[f][mid] - (0.5 * TIME_STEP) * change[f][mid])
        if half % size_f and layer == 0:
            continue
        for d in order:
            to, where = spread(d)
            mine_now = (to < slots) & (to // across * size_f // half == layer) if half % size_f == 0 else to < slots
            if d:

                @pl.when(mine_now)
                def _():
                    remote(window(x_ref, to), cols_ref.at[slot(vector)], s_vec, r_vec, where).start()

    @pl.when(mine < slots)
    def _():
        cols_ref[slot(vector)] = window(x_ref, mine)[...]

    @pl.when(stay)
    def _():
        await_bytes(pool.at[pl.ds(0, parts)], s_cand)

    @pl.when(away)
    def _():
        await_bytes(pool.at[pl.ds(0, 2 * parts)], s_cand)
        await_bytes(anchor.at[:, inner], s_pert)

    await_bytes(out_up, s_give)
    await_bytes(rims, s_edge)

    @pl.when(up_ok)
    def _():
        await_bytes(out_up, s_up)

    @pl.when(dn_ok)
    def _():
        await_bytes(out_dn, s_dn)

    lanes = lax.broadcasted_iota(jnp.int32, (n, 128), 1)
    ranks = lax.broadcasted_iota(jnp.int32, (n, 128), 0)

    @pl.when(mine < slots)
    def _():
        await_bytes(cols_ref.at[pl.ds(0, n - 1)], r_vec)
        gram = jnp.zeros((n, 128), F32)
        for i in range(n):
            total = jnp.sum(cols_ref[...] * cols_ref[slot(i)][None], axis=(1, 2))
            if total.shape[-1] != 128:
                total = total.reshape(n, size_l, 128).sum(axis=1)
            gram = gram + jnp.where(lanes == i, jnp.sum(total, axis=1, keepdims=True), 0.0)
        mine_s[...] = gram

    @pl.when(mine >= slots)
    def _():
        mine_s[...] = jnp.zeros((n, 128), F32)

    if packed:
        row = jnp.sum(pltpu.roll(mine_s[...], 0, 1, stride=n, stride_axis=0), axis=0, keepdims=True)
        mine_v[...] = row
        rank = me * ns + tile
        reach = [(2 * m + c, ds) for m in far_first(lines) for c in range(2) for ds in range(ns) if m or c or ds]
        for dv, ds in reach:
            where = {"vec": paired(me, dv, n), "space": paired(tile, ds, ns)}
            remote(mine_v, gvec.at[rank], s_gv, r_gv, where).start()
        gvec[rank] = row
        await_bytes(gvec.at[pl.ds(0, n * ns - 1)], r_gv)
        row = gvec[0]
        for i in range(1, n * ns):
            row = row + gvec[i]
        gram = pltpu.roll(jnp.broadcast_to(row, (n, 128)), 128 - n * (n - 1), 1, stride=n, stride_axis=0)
    else:
        for d in range(1, ns):
            to = lax.rem(tile + d, ns)
            remote(mine_s, gspace.at[tile], s_gs, r_gs, {"space": to}).start()
        gspace[tile] = mine_s[...]
        await_bytes(gspace.at[pl.ds(0, ns - 1)], r_gs)
        gram = gspace[0]
        for i in range(1, ns):
            gram = gram + gspace[i]
        mine_v[...] = gram
        for d in range(1, n):
            to = lax.rem(me + d, n)
            remote(mine_v, gvec.at[me], s_gv, r_gv, {"vec": to}).start()
        gvec[me] = gram
        await_bytes(gvec.at[pl.ds(0, n - 1)], r_gv)
        gram = gvec[0]
        for i in range(1, n):
            gram = gram + gvec[i]

    a = jnp.where(lanes < n, gram / entries, 0.0) + jnp.where(lanes == ranks + n, 1.0, 0.0)
    diagonal = jnp.ones((n, 1), F32)
    for k in range(n):
        column = a[:, k : k + 1]
        diagonal = jnp.where(ranks[:, :1] == k, column, diagonal)
        factor = jnp.where(ranks[:, :1] > k, column / column[k : k + 1, :], 0.0)
        a = a - factor * a[k : k + 1, :]
    a = a / jnp.sqrt(diagonal)
    upper_ref[...] = jnp.where(lanes >= ranks, a, 0.0)[:, :n]

    @pl.when(mine < slots)
    def _():
        for i in range(n):
            total = a[i : i + 1, n : n + 1][None] * cols_ref[slot(0)]
            for j in range(1, i + 1):
                total = total + a[i : i + 1, n + j : n + j + 1][None] * cols_ref[slot(j)]
            result[i] = total

        for d in order:
            i = paired(vector, d, n)

            @pl.when((me != i) | away)
            def _():
                remote(
                    result.at[i], window(out_ref, mine), s_back, r_back, {"vec": i, "space": block}
                ).start()

        @pl.when(stay)
        def _():
            window(out_ref, mine)[...] = result[me]

    def drain(several, fewer, sem):
        @pl.when(fewer)
        def _():
            await_bytes(result.at[pl.ds(0, several - 1)], sem)

        @pl.when(jnp.logical_not(fewer))
        def _():
            await_bytes(result.at[pl.ds(0, several)], sem)

    drain(slots, stay & (mine < slots), r_back)
    drain(slots, mine < slots, s_vec)

    @pl.when(mine < slots)
    def _():
        drain(n, stay, s_back)

    if packed:
        await_bytes(gvec.at[pl.ds(0, n * ns - 1)], s_gv)
    else:
        await_bytes(gspace.at[pl.ds(0, ns - 1)], s_gs)
        await_bytes(gvec.at[pl.ds(0, n - 1)], s_gv)


def body(n, ns, perturbation, trajectory, step_order):
    pert, traj = perturbation[0], trajectory[0]
    fields, rows, cols = pert.shape
    sections = traj.shape[0]
    chunks, bf = STEPS * sections * (fields // 2), traj.dtype
    packed = n * n <= 128 and n % 8 == 0 and n * ns <= 64
    size_f, size_l = slice_shape(n, fields, cols)
    vmem = pl.BlockSpec(memory_space=pltpu.VMEM)
    hbm = pl.BlockSpec(memory_space=pl.ANY)
    piece = pltpu.VMEM((chunks, rows, cols), bf)
    full = pltpu.VMEM((fields, rows + 2 * HALO, cols), F32)
    slices = pltpu.VMEM((n, size_f, rows, 128 * size_l), F32)
    small = pltpu.VMEM((n, 128), F32)
    dma, one = pltpu.SemaphoreType.DMA, pltpu.SemaphoreType.DMA(())
    out, upper = pl.pallas_call(
        functools.partial(whole_kernel, n, ns, float(fields * rows * cols * ns)),
        out_shape=(pltpu.VMEM(pert.shape, F32), pltpu.VMEM((n, n), F32)),
        in_specs=[hbm, hbm, hbm],
        out_specs=(vmem, vmem),
        scratch_shapes=[
            pltpu.SMEM(step_order.shape, jnp.int32),
            pltpu.VMEM((STEPS * sections, fields, rows + 2 * HALO, cols), bf),
            pltpu.VMEM((2, sections * (fields // 2), rows, cols), bf),
            piece, piece, piece, piece, piece,
            pltpu.VMEM((fields // 2, rows + 4 * HALO, cols), bf),
            pltpu.VMEM((STEPS * sections, fields, 2 * HALO, cols), bf),
            full, pltpu.VMEM((2, *full.shape), F32),
            pltpu.VMEM(pert.shape, F32), slices, slices,
            pltpu.VMEM((ns, n, 128), F32),
            pltpu.VMEM((n * ns, 1, 128) if packed else (n, n, 128), F32),
            small,
            pltpu.VMEM((1, 128), F32) if packed else small,
            one, dma((sections * (fields // 2),)), dma((chunks,)), dma((chunks,)), dma((STEPS * sections,)),
            one, one, one, one, one, one,
            one, one, one, one, one, one, one, one, one, one, one,
        ],
        compiler_params=pltpu.CompilerParams(collective_id=0, has_side_effects=True),
        name="whole",
    )(step_order, traj, pert)

    def finish(back_ref, upper_ref, out_ref, factor_ref, sems):
        copies = [
            pltpu.make_async_copy(back_ref, out_ref, sems.at[0]),
            pltpu.make_async_copy(upper_ref, factor_ref, sems.at[1]),
        ]
        for copy in copies:
            copy.start()
        for copy in copies:
            copy.wait()

    out, factor = pl.pallas_call(
        finish,
        out_shape=(jax.ShapeDtypeStruct(pert.shape, F32), jax.ShapeDtypeStruct((n, n), F32)),
        in_specs=[vmem, vmem],
        out_specs=(hbm, hbm),
        scratch_shapes=[dma((2,))],
        name="finish",
    )(
        pltpu.with_memory_space_constraint(out, pltpu.VMEM),
        pltpu.with_memory_space_constraint(upper, pltpu.VMEM),
    )
    return out[None], factor


def solution(mesh):
    n, ns = mesh.shape["vec"], mesh.shape["space"]
    in_specs = (P("vec", None, "space", None), P("vec", None, None, "space", None), P())
    out_specs = (P("vec", None, "space", None), P())
    return jax.shard_map(
        functools.partial(body, n, ns), mesh=mesh, in_specs=in_specs, out_specs=out_specs, check_vma=False
    )
```

```python
import functools

import jax
import jax.numpy as jnp
from jax import lax
from jax.experimental import pallas as pl
from jax.experimental.pallas import tpu as pltpu
from jax.sharding import PartitionSpec as P

STEPS = 2
SECTIONS = 3
LAG_UP = 6
LAG_DN = 6
RUN_LAG_END = 8
RUN_LAG_MID = 17
HALO = 8

GRAVITY_TOP = 1.0
GRAVITY_LOW = 0.5
DEPTH_TOP = 1.0
DEPTH_LOW = 1.0
CORIOLIS = 0.3
TIME_STEP = 0.25

MESH = pl.DeviceIdType.MESH
F32 = jnp.float32


def remote(src, dst, send, recv, target):
    return pltpu.make_async_remote_copy(
        src_ref=src, dst_ref=dst, send_sem=send, recv_sem=recv, device_id=target, device_id_type=MESH
    )


def await_bytes(ref, sem):
    pltpu.make_async_copy(ref, ref, sem).wait()


def twice_dx(field):
    count = field.shape[0]
    return pltpu.roll(field, count - 1, 0) - pltpu.roll(field, 1, 0)


def twice_dy(field):
    count = field.shape[1]
    return pltpu.roll(field, count - 1, 1) - pltpu.roll(field, 1, 1)


def tangent(layer, base, state, top, low):
    pressure = GRAVITY_TOP * (top + low)
    if layer:
        pressure = pressure + GRAVITY_LOW * low
    depth = base[0] + (DEPTH_TOP, DEPTH_LOW)[layer]
    u, v = base[1], base[2]
    dh, du, dv = state
    return [
        twice_dx(depth * du + dh * u) + twice_dy(depth * dv + dh * v),
        (u * twice_dx(du) + du * twice_dx(u)) + (v * twice_dy(du) + dv * twice_dy(u))
        + twice_dx(pressure) - (2 * CORIOLIS) * dv,
        (u * twice_dx(dv) + du * twice_dx(v)) + (v * twice_dy(dv) + dv * twice_dy(v))
        + twice_dy(pressure) + (2 * CORIOLIS) * du,
    ]


def slice_shape(n, fields, cols):
    lanes = cols // 128
    best = None
    for f in range(1, fields + 1):
        for l in range(1, lanes + 1):
            if fields % f or lanes % l or (fields // f) * (lanes // l) > n:
                continue
            if best is None or f * l < best[0] * best[1]:
                best = (f, l)
    return best


def paired(value, mask, count):
    if count & (count - 1):
        return lax.rem(value + mask, count)
    made, bit = 0, 1
    while bit < count:
        digit = lax.rem(lax.div(value, bit), 2)
        made = made + bit * (1 - digit if mask & bit else digit)
        bit *= 2
    return made


def far_first(count):
    return sorted(range(count), key=lambda m: (-m.bit_length(), m))


def whole_kernel(
    n, ns, entries, order_in, traj_ref, pert_ref,
    out_ref, upper_ref,
    order_ref, main, cand, in_up, in_dn, out_up, out_dn, pool, fresh, rims, anchor, work,
    x_ref, cols_ref, result, gspace, gvec, mine_s, mine_v,
    r_order, r_cand, r_up, r_dn, r_sec, r_pert, r_side, r_vec, r_gs, r_gv, r_back,
    s_cand, s_pert, s_side, s_up, s_dn, s_give, s_edge, s_vec, s_gs, s_gv, s_back,
):
    me = lax.axis_index("vec")
    tile = lax.axis_index("space")
    fields, rows, cols = pert_ref.shape
    half = fields // 2
    per = rows // HALO
    parts = SECTIONS * per
    chunks = STEPS * parts
    lines, places = n // 2, ns // 2
    side, line = lax.rem(me, 2), me // 2
    core, place = lax.rem(tile, 2), tile // 2
    flip = lax.rem(place, 2)

    def differs(a, b):
        return a + b - 2 * a * b

    home = differs(side, flip)
    stay = core == home
    away = core != home
    block = 2 * place + home
    vector = 2 * line + differs(core, flip)
    sibling = {"space": 2 * place + 1 - core}
    up_ok = line < lines - 1
    dn_ok = line > 0

    def worker(v, t):
        p = t // 2
        turn = lax.rem(p, 2)
        return {
            "vec": 2 * (v // 2) + differs(lax.rem(t, 2), turn),
            "space": 2 * p + differs(lax.rem(v, 2), turn),
        }

    barrier = pltpu.get_barrier_semaphore()
    near = sorted({0, 1 % places, places - 1})
    count = 0
    for across in range(2):
        for step in near:
            for c in range(2):
                if (across == 0 and step == 0 and c == 0) or (across and step):
                    continue
                where = {
                    "vec": me + across * (1 - 2 * side),
                    "space": 2 * lax.rem(place + step, places) + lax.rem(core + c, 2),
                }
                pl.semaphore_signal(barrier, inc=1, device_id=where, device_id_type=MESH)
                count += 1

    @pl.when(up_ok)
    def _():
        pl.semaphore_signal(barrier, inc=1, device_id={"vec": me + 2}, device_id_type=MESH)

    @pl.when(dn_ok)
    def _():
        pl.semaphore_signal(barrier, inc=1, device_id={"vec": me - 2}, device_id_type=MESH)

    inner = pl.ds(HALO, rows)

    def band(w):
        return pl.multiple_of(HALO * jnp.where(w == 0, 0, jnp.where(w == 1, per - 1, w - 1)), HALO)

    def origin(p, layer):
        return traj_ref.at[lax.div(p, per), pl.ds(half * layer, half), pl.ds(band(lax.rem(p, per)), HALO)]

    order_copy = pltpu.make_async_copy(order_in, order_ref, r_order)
    order_copy.start()

    @pl.when(stay)
    def _():
        @pl.loop(0, parts)
        def _(p):
            pltpu.make_async_copy(origin(p, core), cand.at[0, p], r_cand.at[p]).start()

        pltpu.make_async_copy(pert_ref, anchor.at[:, inner], r_pert).start()

    pl.semaphore_wait(barrier, count + up_ok.astype(jnp.int32) + dn_ok.astype(jnp.int32))

    other = me + 1 - 2 * side

    @pl.when(stay)
    def _():
        @pl.loop(0, parts)
        def _(p):
            remote(
                origin(p, 1 - core), cand.at[0, p], s_cand, r_cand.at[p], sibling
            ).start()

    @pl.when(away)
    def _():
        @pl.loop(0, parts)
        def _(p):
            for c in range(2):
                remote(
                    origin(p, c), cand.at[1, p], s_cand, r_cand.at[p],
                    {"vec": other, "space": 2 * place + c},
                ).start()

    @pl.when(away)
    def _():
        remote(
            pert_ref, anchor.at[:, inner], s_pert, r_pert,
            {"vec": other, "space": 2 * place + 1 - core},
        ).start()

    def go_up(c):
        return remote(out_up.at[c], in_up.at[c], s_up, r_up.at[c], {"vec": me + 2})

    def go_dn(c):
        return remote(out_dn.at[c], in_dn.at[c], s_dn, r_dn.at[c], {"vec": me - 2})

    def owner_of(c):
        return jnp.where(c >= parts, order_ref[1], order_ref[0])

    def candidate(c):
        p = lax.rem(c, parts)
        return jnp.where(owner_of(c) == me, cand[0, p], cand[1, p])

    def inside(c):
        return (c >= 0) & (c < chunks)

    first_block = worker(vector, lax.rem(block + 1, ns))
    last_block = worker(vector, lax.rem(block + ns - 1, ns))
    own_layer = pl.ds(half * core, half)

    run_lag = jnp.where(up_ok & dn_ok, RUN_LAG_MID, RUN_LAG_END)
    up_lag = LAG_UP * line
    dn_lag = LAG_DN * (lines - 1 - line)
    near_lag = jnp.where(up_ok & dn_ok, jnp.minimum(up_lag, dn_lag), 0)
    far_lag = jnp.maximum(up_lag, dn_lag)
    most = max(
        max(LAG_UP * l, LAG_DN * (lines - 1 - l)) + (RUN_LAG_MID if 0 < l < lines - 1 else RUN_LAG_END)
        for l in range(lines)
    )

    def rates(number, layer):
        now = lax.rem(number, 2)
        at = half * layer
        base = [main[number, at + f].astype(F32) for f in range(half)]
        state = [work[now, at + f] for f in range(half)]
        top = state[0] if layer == 0 else work[now, 0]
        low = state[0] if layer == 1 else work[now, half]
        return state, tangent(layer, base, state, top, low)

    def advance(number, layer):
        section = lax.rem(number, SECTIONS)
        state, change = rates(number, layer)
        keep = jnp.where(section == 0, 0.0, jnp.where(section == 1, 0.75, 1.0 / 3.0)).astype(F32)
        take = jnp.where(section == 0, 1.0, jnp.where(section == 1, 0.25, 2.0 / 3.0)).astype(F32)
        for f in range(half):
            at = half * layer + f
            work[1 - lax.rem(number, 2), at] = keep * anchor[at] + take * (state[f] - (0.5 * TIME_STEP) * change[f])

        @pl.when(section == SECTIONS - 1)
        def _():
            for f in range(half):
                at = half * layer + f
                anchor[at] = work[1 - lax.rem(number, 2), at]

    order_copy.wait()

    @pl.loop(0, most + chunks - per + 1)
    def _(t):
        c_pair = t - near_lag
        c_up = t - up_lag
        c_dn = t - dn_lag
        c_fin = t - far_lag
        c_run = c_fin - run_lag

        @pl.when((c_pair >= 0) & (c_pair < parts))
        def _():
            await_bytes(cand.at[:, c_pair], r_cand.at[c_pair])

        @pl.when(inside(c_up))
        def _():
            @pl.when(dn_ok)
            def _():
                go_up(c_up).wait_recv()

            @pl.when(up_ok)
            def _():
                here = lax.div(owner_of(c_up), 2) == line
                out_up[c_up] = jnp.where(here, candidate(c_up), in_up[c_up])
                go_up(c_up).start()

        @pl.when(inside(c_dn))
        def _():
            @pl.when(up_ok)
            def _():
                go_dn(c_dn).wait_recv()

            @pl.when(dn_ok)
            def _():
                here = lax.div(owner_of(c_dn), 2) == line
                out_dn[c_dn] = jnp.where(here, candidate(c_dn), in_dn[c_dn])
                go_dn(c_dn).start()

        @pl.when(inside(c_fin))
        def _():
            at = lax.div(owner_of(c_fin), 2)
            q, w = lax.div(c_fin, per), lax.rem(c_fin, per)
            spot = main.at[q, own_layer, pl.ds(HALO + band(w), HALO)]
            spot[...] = jnp.where(
                at == line, candidate(c_fin), jnp.where(at < line, in_up[c_fin], in_dn[c_fin])
            )
            remote(spot, spot, s_give, r_sec.at[q], sibling).start()

            for turn, target, src, dst in ((0, last_block, HALO, HALO + rows), (1, first_block, rows, 0)):

                @pl.when(w == turn)
                def _():
                    for c in range(2):
                        remote(
                            main.at[q, own_layer, pl.ds(src, HALO)],
                            main.at[q, own_layer, pl.ds(dst, HALO)],
                            s_edge, r_sec.at[q],
                            {"vec": target["vec"], "space": 2 * (target["space"] // 2) + c},
                        ).start()

        @pl.when(c_fin == per - 1)
        def _():
            await_bytes(anchor.at[:, inner], r_pert)
            for target, src, dst in ((first_block, rows, 0), (last_block, HALO, HALO + rows)):
                remote(
                    anchor.at[:, pl.ds(src, HALO)], anchor.at[:, pl.ds(dst, HALO)], s_side, r_side, target
                ).start()

        @pl.when(c_run == per - 1)
        def _():
            await_bytes(anchor.at[:, pl.ds(0, 2 * HALO)], r_side)
            await_bytes(anchor.at[:, pl.ds(0, 2 * HALO)], s_side)
            work[0] = anchor[...]

        @pl.when((c_run >= per - 1) & (c_run < chunks - 1) & (lax.rem(c_run, per) == per - 1))
        def _():
            number = lax.div(c_run, per)
            await_bytes(fresh, r_sec.at[number])
            advance(number, 0)

        @pl.when((c_run >= per) & (c_run < chunks) & (lax.rem(c_run, per) == 0))
        def _():
            advance(lax.div(c_run, per) - 1, 1)

    size_f, size_l = slice_shape(n, fields, cols)
    across = cols // (128 * size_l)
    slots = (fields // size_f) * across
    mine = 2 * line + core
    packed = n * n <= 128 and n % 8 == 0 and n * ns <= 64

    def slot(v):
        return n - 1 - v if packed else v

    def window(ref, j):
        f = pl.multiple_of(lax.div(j, across) * size_f, size_f)
        l = pl.multiple_of(lax.rem(j, across) * (128 * size_l), 128 * size_l)
        return ref.at[pl.ds(f, size_f), :, pl.ds(l, 128 * size_l)]

    def spread(d):
        to = paired(mine, d, n)
        return to, {"vec": 2 * (to // 2) + side, "space": 2 * place + lax.rem(to, 2)}

    order = [2 * m + c for m in far_first(lines) for c in range(2)]
    final = STEPS * SECTIONS - 1
    await_bytes(fresh, r_sec.at[final])
    mid = slice(HALO, HALO + rows)
    for layer in range(2):
        state, change = rates(final, layer)
        for f in range(half):
            at = half * layer + f
            x_ref[at] = anchor[at, mid] * (1.0 / 3.0) + (2.0 / 3.0) * (state[f][mid] - (0.5 * TIME_STEP) * change[f][mid])
        if half % size_f and layer == 0:
            continue
        for d in order:
            to, where = spread(d)
            mine_now = (to < slots) & (to // across * size_f // half == layer) if half % size_f == 0 else to < slots
            if d:

                @pl.when(mine_now)
                def _():
                    remote(window(x_ref, to), cols_ref.at[slot(vector)], s_vec, r_vec, where).start()

    @pl.when(mine < slots)
    def _():
        cols_ref[slot(vector)] = window(x_ref, mine)[...]

    @pl.when(stay)
    def _():
        await_bytes(pool.at[pl.ds(0, parts)], s_cand)

    @pl.when(away)
    def _():
        await_bytes(pool.at[pl.ds(0, 2 * parts)], s_cand)
        await_bytes(anchor.at[:, inner], s_pert)

    await_bytes(out_up, s_give)
    await_bytes(rims, s_edge)

    @pl.when(up_ok)
    def _():
        await_bytes(out_up, s_up)

    @pl.when(dn_ok)
    def _():
        await_bytes(out_dn, s_dn)

    lanes = lax.broadcasted_iota(jnp.int32, (n, 128), 1)
    ranks = lax.broadcasted_iota(jnp.int32, (n, 128), 0)

    @pl.when(mine < slots)
    def _():
        await_bytes(cols_ref.at[pl.ds(0, n - 1)], r_vec)
        gram = jnp.zeros((n, 128), F32)
        for i in range(n):
            total = jnp.sum(cols_ref[...] * cols_ref[slot(i)][None], axis=(1, 2))
            if total.shape[-1] != 128:
                total = total.reshape(n, size_l, 128).sum(axis=1)
            gram = gram + jnp.where(lanes == i, jnp.sum(total, axis=1, keepdims=True), 0.0)
        mine_s[...] = gram

    @pl.when(mine >= slots)
    def _():
        mine_s[...] = jnp.zeros((n, 128), F32)

    if packed:
        row = jnp.sum(pltpu.roll(mine_s[...], 0, 1, stride=n, stride_axis=0), axis=0, keepdims=True)
        mine_v[...] = row
        rank = me * ns + tile
        reach = [(2 * m + c, ds) for m in far_first(lines) for c in range(2) for ds in range(ns) if m or c or ds]
        for dv, ds in reach:
            where = {"vec": paired(me, dv, n), "space": paired(tile, ds, ns)}
            remote(mine_v, gvec.at[rank], s_gv, r_gv, where).start()
        gvec[rank] = row
        await_bytes(gvec.at[pl.ds(0, n * ns - 1)], r_gv)
        row = gvec[0]
        for i in range(1, n * ns):
            row = row + gvec[i]
        gram = pltpu.roll(jnp.broadcast_to(row, (n, 128)), 128 - n * (n - 1), 1, stride=n, stride_axis=0)
    else:
        for d in range(1, ns):
            to = lax.rem(tile + d, ns)
            remote(mine_s, gspace.at[tile], s_gs, r_gs, {"space": to}).start()
        gspace[tile] = mine_s[...]
        await_bytes(gspace.at[pl.ds(0, ns - 1)], r_gs)
        gram = gspace[0]
        for i in range(1, ns):
            gram = gram + gspace[i]
        mine_v[...] = gram
        for d in range(1, n):
            to = lax.rem(me + d, n)
            remote(mine_v, gvec.at[me], s_gv, r_gv, {"vec": to}).start()
        gvec[me] = gram
        await_bytes(gvec.at[pl.ds(0, n - 1)], r_gv)
        gram = gvec[0]
        for i in range(1, n):
            gram = gram + gvec[i]

    a = jnp.where(lanes < n, gram / entries, 0.0) + jnp.where(lanes == ranks + n, 1.0, 0.0)
    diagonal = jnp.ones((n, 1), F32)
    for k in range(n):
        column = a[:, k : k + 1]
        diagonal = jnp.where(ranks[:, :1] == k, column, diagonal)
        factor = jnp.where(ranks[:, :1] > k, column / column[k : k + 1, :], 0.0)
        a = a - factor * a[k : k + 1, :]
    a = a / jnp.sqrt(diagonal)
    upper_ref[...] = jnp.where(lanes >= ranks, a, 0.0)[:, :n]

    @pl.when(mine < slots)
    def _():
        for i in range(n):
            total = a[i : i + 1, n : n + 1][None] * cols_ref[slot(0)]
            for j in range(1, i + 1):
                total = total + a[i : i + 1, n + j : n + j + 1][None] * cols_ref[slot(j)]
            result[i] = total

        for d in order:
            i = paired(vector, d, n)

            @pl.when((me != i) | away)
            def _():
                remote(
                    result.at[i], window(out_ref, mine), s_back, r_back, {"vec": i, "space": block}
                ).start()

        @pl.when(stay)
        def _():
            window(out_ref, mine)[...] = result[me]

    def drain(several, fewer, sem):
        @pl.when(fewer)
        def _():
            await_bytes(result.at[pl.ds(0, several - 1)], sem)

        @pl.when(jnp.logical_not(fewer))
        def _():
            await_bytes(result.at[pl.ds(0, several)], sem)

    drain(slots, stay & (mine < slots), r_back)
    drain(slots, mine < slots, s_vec)

    @pl.when(mine < slots)
    def _():
        drain(n, stay, s_back)

    if packed:
        await_bytes(gvec.at[pl.ds(0, n * ns - 1)], s_gv)
    else:
        await_bytes(gspace.at[pl.ds(0, ns - 1)], s_gs)
        await_bytes(gvec.at[pl.ds(0, n - 1)], s_gv)


def body(n, ns, perturbation, trajectory, step_order):
    pert, traj = perturbation[0], trajectory[0]
    fields, rows, cols = pert.shape
    sections = traj.shape[0]
    parts, bf = sections * (rows // HALO), traj.dtype
    chunks, layer = STEPS * parts, fields // 2
    packed = n * n <= 128 and n % 8 == 0 and n * ns <= 64
    size_f, size_l = slice_shape(n, fields, cols)
    vmem = pl.BlockSpec(memory_space=pltpu.VMEM)
    hbm = pl.BlockSpec(memory_space=pl.ANY)
    piece = pltpu.VMEM((chunks, layer, HALO, cols), bf)
    full = pltpu.VMEM((fields, rows + 2 * HALO, cols), F32)
    slices = pltpu.VMEM((n, size_f, rows, 128 * size_l), F32)
    small = pltpu.VMEM((n, 128), F32)
    dma, one = pltpu.SemaphoreType.DMA, pltpu.SemaphoreType.DMA(())
    out, upper = pl.pallas_call(
        functools.partial(whole_kernel, n, ns, float(fields * rows * cols * ns)),
        out_shape=(pltpu.VMEM(pert.shape, F32), pltpu.VMEM((n, n), F32)),
        in_specs=[hbm, hbm, hbm],
        out_specs=(vmem, vmem),
        scratch_shapes=[
            pltpu.SMEM(step_order.shape, jnp.int32),
            pltpu.VMEM((STEPS * sections, fields, rows + 2 * HALO, cols), bf),
            pltpu.VMEM((2, parts, layer, HALO, cols), bf),
            piece, piece, piece, piece, piece,
            pltpu.VMEM((fields // 2, rows + 4 * HALO, cols), bf),
            pltpu.VMEM((STEPS * sections, fields, 2 * HALO, cols), bf),
            full, pltpu.VMEM((2, *full.shape), F32),
            pltpu.VMEM(pert.shape, F32), slices, slices,
            pltpu.VMEM((ns, n, 128), F32),
            pltpu.VMEM((n * ns, 1, 128) if packed else (n, n, 128), F32),
            small,
            pltpu.VMEM((1, 128), F32) if packed else small,
            one, dma((parts,)), dma((chunks,)), dma((chunks,)), dma((STEPS * sections,)),
            one, one, one, one, one, one,
            one, one, one, one, one, one, one, one, one, one, one,
        ],
        compiler_params=pltpu.CompilerParams(collective_id=0, has_side_effects=True),
        name="whole",
    )(step_order, traj, pert)

    def finish(back_ref, upper_ref, out_ref, factor_ref, sems):
        copies = [
            pltpu.make_async_copy(back_ref, out_ref, sems.at[0]),
            pltpu.make_async_copy(upper_ref, factor_ref, sems.at[1]),
        ]
        for copy in copies:
            copy.start()
        for copy in copies:
            copy.wait()

    out, factor = pl.pallas_call(
        finish,
        out_shape=(jax.ShapeDtypeStruct(pert.shape, F32), jax.ShapeDtypeStruct((n, n), F32)),
        in_specs=[vmem, vmem],
        out_specs=(hbm, hbm),
        scratch_shapes=[dma((2,))],
        name="finish",
    )(
        pltpu.with_memory_space_constraint(out, pltpu.VMEM),
        pltpu.with_memory_space_constraint(upper, pltpu.VMEM),
    )
    return out[None], factor


def solution(mesh):
    n, ns = mesh.shape["vec"], mesh.shape["space"]
    in_specs = (P("vec", None, "space", None), P("vec", None, None, "space", None), P())
    out_specs = (P("vec", None, "space", None), P())
    return jax.shard_map(
        functools.partial(body, n, ns), mesh=mesh, in_specs=in_specs, out_specs=out_specs, check_vma=False
    )
```

```python
import functools

import jax
import jax.numpy as jnp
from jax import lax
from jax.experimental import pallas as pl
from jax.experimental.pallas import tpu as pltpu
from jax.sharding import PartitionSpec as P

STEPS = 2
SECTIONS = 3
LAG_UP = 6
LAG_DN = 6
RUN_LAG_END = 8
RUN_LAG_MID = 17
HALO = 8

GRAVITY_TOP = 1.0
GRAVITY_LOW = 0.5
DEPTH_TOP = 1.0
DEPTH_LOW = 1.0
CORIOLIS = 0.3
TIME_STEP = 0.25

MESH = pl.DeviceIdType.MESH
F32 = jnp.float32


def remote(src, dst, send, recv, target):
    return pltpu.make_async_remote_copy(
        src_ref=src, dst_ref=dst, send_sem=send, recv_sem=recv, device_id=target, device_id_type=MESH
    )


def await_bytes(ref, sem):
    pltpu.make_async_copy(ref, ref, sem).wait()


def twice_dx(field):
    count = field.shape[0]
    return pltpu.roll(field, count - 1, 0) - pltpu.roll(field, 1, 0)


def twice_dy(field):
    count = field.shape[1]
    return pltpu.roll(field, count - 1, 1) - pltpu.roll(field, 1, 1)


def tangent(layer, base, state, top, low):
    pressure = GRAVITY_TOP * (top + low)
    if layer:
        pressure = pressure + GRAVITY_LOW * low
    depth = base[0] + (DEPTH_TOP, DEPTH_LOW)[layer]
    u, v = base[1], base[2]
    dh, du, dv = state
    return [
        twice_dx(depth * du + dh * u) + twice_dy(depth * dv + dh * v),
        (u * twice_dx(du) + du * twice_dx(u)) + (v * twice_dy(du) + dv * twice_dy(u))
        + twice_dx(pressure) - (2 * CORIOLIS) * dv,
        (u * twice_dx(dv) + du * twice_dx(v)) + (v * twice_dy(dv) + dv * twice_dy(v))
        + twice_dy(pressure) + (2 * CORIOLIS) * du,
    ]


def slice_shape(n, fields, cols):
    lanes = cols // 128
    best = None
    for f in range(1, fields + 1):
        for l in range(1, lanes + 1):
            if fields % f or lanes % l or (fields // f) * (lanes // l) > n:
                continue
            if best is None or f * l < best[0] * best[1]:
                best = (f, l)
    return best


def paired(value, mask, count):
    if count & (count - 1):
        return lax.rem(value + mask, count)
    made, bit = 0, 1
    while bit < count:
        digit = lax.rem(lax.div(value, bit), 2)
        made = made + bit * (1 - digit if mask & bit else digit)
        bit *= 2
    return made


def far_first(count):
    return sorted(range(count), key=lambda m: (-m.bit_length(), m))


def whole_kernel(
    n, ns, entries, order_in, traj_ref, pert_ref,
    out_ref, upper_ref,
    order_ref, main, cand, in_up, in_dn, out_up, out_dn, pool, fresh, rims, anchor, work,
    x_ref, cols_ref, result, gspace, gvec, mine_s, mine_v,
    r_order, r_cand, r_up, r_dn, r_sec, r_pert, r_side, r_vec, r_gs, r_gv, r_back,
    s_cand, s_pert, s_side, s_up, s_dn, s_give, s_edge, s_vec, s_gs, s_gv, s_back,
):
    me = lax.axis_index("vec")
    tile = lax.axis_index("space")
    fields, rows, cols = pert_ref.shape
    half = fields // 2
    per = rows // HALO
    parts = SECTIONS * per
    chunks = STEPS * parts
    lines, places = n // 2, ns // 2
    side, line = lax.rem(me, 2), me // 2
    core, place = lax.rem(tile, 2), tile // 2
    flip = lax.rem(place, 2)

    def differs(a, b):
        return a + b - 2 * a * b

    home = differs(side, flip)
    stay = core == home
    away = core != home
    block = 2 * place + home
    vector = 2 * line + differs(core, flip)
    sibling = {"space": 2 * place + 1 - core}
    up_ok = line < lines - 1
    dn_ok = line > 0

    def worker(v, t):
        p = t // 2
        turn = lax.rem(p, 2)
        return {
            "vec": 2 * (v // 2) + differs(lax.rem(t, 2), turn),
            "space": 2 * p + differs(lax.rem(v, 2), turn),
        }

    barrier = pltpu.get_barrier_semaphore()
    near = sorted({0, 1 % places, places - 1})
    count = 0
    for across in range(2):
        for step in near:
            for c in range(2):
                if (across == 0 and step == 0 and c == 0) or (across and step):
                    continue
                where = {
                    "vec": me + across * (1 - 2 * side),
                    "space": 2 * lax.rem(place + step, places) + lax.rem(core + c, 2),
                }
                pl.semaphore_signal(barrier, inc=1, device_id=where, device_id_type=MESH)
                count += 1

    @pl.when(up_ok)
    def _():
        pl.semaphore_signal(barrier, inc=1, device_id={"vec": me + 2}, device_id_type=MESH)

    @pl.when(dn_ok)
    def _():
        pl.semaphore_signal(barrier, inc=1, device_id={"vec": me - 2}, device_id_type=MESH)

    inner = pl.ds(HALO, rows)

    def band(w):
        return pl.multiple_of(HALO * jnp.where(w == 0, 0, jnp.where(w == 1, per - 1, w - 1)), HALO)

    def origin(p, layer):
        return traj_ref.at[lax.div(p, per), pl.ds(half * layer, half), pl.ds(band(lax.rem(p, per)), HALO)]

    order_copy = pltpu.make_async_copy(order_in, order_ref, r_order)
    order_copy.start()

    @pl.when(stay)
    def _():
        @pl.loop(0, parts)
        def _(p):
            pltpu.make_async_copy(origin(p, core), cand.at[0, p], r_cand.at[p]).start()

        pltpu.make_async_copy(pert_ref, anchor.at[:, inner], r_pert).start()

    pl.semaphore_wait(barrier, count + up_ok.astype(jnp.int32) + dn_ok.astype(jnp.int32))

    other = me + 1 - 2 * side

    @pl.when(stay)
    def _():
        @pl.loop(0, parts)
        def _(p):
            remote(
                origin(p, 1 - core), cand.at[0, p], s_cand, r_cand.at[p], sibling
            ).start()

    @pl.when(away)
    def _():
        @pl.loop(0, parts)
        def _(p):
            for c in range(2):
                remote(
                    origin(p, c), cand.at[1, p], s_cand, r_cand.at[p],
                    {"vec": other, "space": 2 * place + c},
                ).start()

    @pl.when(away)
    def _():
        remote(
            pert_ref, anchor.at[:, inner], s_pert, r_pert,
            {"vec": other, "space": 2 * place + 1 - core},
        ).start()

    def go_up(c):
        return remote(out_up.at[c], in_up.at[c], s_up, r_up.at[c], {"vec": me + 2})

    def go_dn(c):
        return remote(out_dn.at[c], in_dn.at[c], s_dn, r_dn.at[c], {"vec": me - 2})

    def owner_of(c):
        return jnp.where(c >= parts, order_ref[1], order_ref[0])

    def candidate(c):
        p = lax.rem(c, parts)
        return jnp.where(owner_of(c) == me, cand[0, p], cand[1, p])

    def inside(c):
        return (c >= 0) & (c < chunks)

    first_block = worker(vector, lax.rem(block + 1, ns))
    last_block = worker(vector, lax.rem(block + ns - 1, ns))
    own_layer = pl.ds(half * core, half)

    run_lag = jnp.where(up_ok & dn_ok, RUN_LAG_MID, RUN_LAG_END)
    up_lag = LAG_UP * line
    dn_lag = LAG_DN * (lines - 1 - line)
    near_lag = jnp.where(up_ok & dn_ok, jnp.minimum(up_lag, dn_lag), 0)
    far_lag = jnp.maximum(up_lag, dn_lag)
    most = max(
        max(LAG_UP * l, LAG_DN * (lines - 1 - l)) + (RUN_LAG_MID if 0 < l < lines - 1 else RUN_LAG_END)
        for l in range(lines)
    )

    def rates(number, layer):
        now = lax.rem(number, 2)
        at = half * layer
        base = [main[number, at + f].astype(F32) for f in range(half)]
        state = [work[now, at + f] for f in range(half)]
        top = state[0] if layer == 0 else work[now, 0]
        low = state[0] if layer == 1 else work[now, half]
        return state, tangent(layer, base, state, top, low)

    def advance(number, layer):
        section = lax.rem(number, SECTIONS)
        state, change = rates(number, layer)
        keep = jnp.where(section == 0, 0.0, jnp.where(section == 1, 0.75, 1.0 / 3.0)).astype(F32)
        take = jnp.where(section == 0, 1.0, jnp.where(section == 1, 0.25, 2.0 / 3.0)).astype(F32)
        for f in range(half):
            at = half * layer + f
            work[1 - lax.rem(number, 2), at] = keep * anchor[at] + take * (state[f] - (0.5 * TIME_STEP) * change[f])

        @pl.when(section == SECTIONS - 1)
        def _():
            for f in range(half):
                at = half * layer + f
                anchor[at] = work[1 - lax.rem(number, 2), at]

    order_copy.wait()

    @pl.loop(0, most + chunks - per + 1)
    def _(t):
        c_pair = t - near_lag
        c_up = t - up_lag
        c_dn = t - dn_lag
        c_fin = t - far_lag
        c_run = c_fin - run_lag

        @pl.when((c_pair >= 0) & (c_pair < parts))
        def _():
            await_bytes(cand.at[:, c_pair], r_cand.at[c_pair])

        @pl.when(inside(c_up))
        def _():
            @pl.when(dn_ok)
            def _():
                go_up(c_up).wait_recv()

            @pl.when(up_ok)
            def _():
                here = lax.div(owner_of(c_up), 2) == line
                out_up[c_up] = jnp.where(here, candidate(c_up), in_up[c_up])
                go_up(c_up).start()

        @pl.when(inside(c_dn))
        def _():
            @pl.when(up_ok)
            def _():
                go_dn(c_dn).wait_recv()

            @pl.when(dn_ok)
            def _():
                here = lax.div(owner_of(c_dn), 2) == line
                out_dn[c_dn] = jnp.where(here, candidate(c_dn), in_dn[c_dn])
                go_dn(c_dn).start()

        @pl.when(inside(c_fin))
        def _():
            at = lax.div(owner_of(c_fin), 2)
            q, w = lax.div(c_fin, per), lax.rem(c_fin, per)
            spot = main.at[q, own_layer, pl.ds(HALO + band(w), HALO)]
            spot[...] = jnp.where(
                at == line, candidate(c_fin), jnp.where(at < line, in_up[c_fin], in_dn[c_fin])
            )
            remote(spot, spot, s_give, r_sec.at[q], sibling).start()

            for turn, target, src, dst in ((0, last_block, HALO, HALO + rows), (1, first_block, rows, 0)):

                @pl.when(w == turn)
                def _():
                    for c in range(2):
                        remote(
                            main.at[q, own_layer, pl.ds(src, HALO)],
                            main.at[q, own_layer, pl.ds(dst, HALO)],
                            s_edge, r_sec.at[q],
                            {"vec": target["vec"], "space": 2 * (target["space"] // 2) + c},
                        ).start()

        @pl.when(c_fin == per - 1)
        def _():
            await_bytes(anchor.at[:, inner], r_pert)
            for target, src, dst in ((first_block, rows, 0), (last_block, HALO, HALO + rows)):
                remote(
                    anchor.at[:, pl.ds(src, HALO)], anchor.at[:, pl.ds(dst, HALO)], s_side, r_side, target
                ).start()

        @pl.when(c_run == per - 1)
        def _():
            await_bytes(anchor.at[:, pl.ds(0, 2 * HALO)], r_side)
            await_bytes(anchor.at[:, pl.ds(0, 2 * HALO)], s_side)
            work[0] = anchor[...]

        @pl.when((c_run >= per - 1) & (c_run < chunks - 1) & (lax.rem(c_run, per) == per - 1))
        def _():
            number = lax.div(c_run, per)
            await_bytes(fresh, r_sec.at[number])
            advance(number, 0)

        @pl.when((c_run >= per) & (c_run < chunks) & (lax.rem(c_run, per) == 0))
        def _():
            advance(lax.div(c_run, per) - 1, 1)

    size_f, size_l = slice_shape(n, fields, cols)
    across = cols // (128 * size_l)
    slots = (fields // size_f) * across

    def share(v):
        return lines * lax.rem(v, 2) + lax.div(v, 2)

    mine = share(2 * line + core)
    packed = n * n <= 128 and n % 8 == 0 and n * ns <= 64

    def slot(v):
        return n - 1 - v if packed else v

    def window(ref, j):
        f = pl.multiple_of(lax.div(j, across) * size_f, size_f)
        l = pl.multiple_of(lax.rem(j, across) * (128 * size_l), 128 * size_l)
        return ref.at[pl.ds(f, size_f), :, pl.ds(l, 128 * size_l)]

    def spread(d):
        to = paired(2 * line + core, d, n)
        return share(to), {"vec": 2 * (to // 2) + side, "space": 2 * place + lax.rem(to, 2)}

    order = [2 * m + c for m in far_first(lines) for c in range(2)]
    final = STEPS * SECTIONS - 1
    await_bytes(fresh, r_sec.at[final])
    mid = slice(HALO, HALO + rows)
    for layer in range(2):
        state, change = rates(final, layer)
        for f in range(half):
            at = half * layer + f
            x_ref[at] = anchor[at, mid] * (1.0 / 3.0) + (2.0 / 3.0) * (state[f][mid] - (0.5 * TIME_STEP) * change[f][mid])
        if half % size_f and layer == 0:
            continue
        for d in order:
            to, where = spread(d)
            mine_now = (to < slots) & (to // across * size_f // half == layer) if half % size_f == 0 else to < slots
            if d:

                @pl.when(mine_now)
                def _():
                    remote(window(x_ref, to), cols_ref.at[slot(vector)], s_vec, r_vec, where).start()

    @pl.when(mine < slots)
    def _():
        cols_ref[slot(vector)] = window(x_ref, mine)[...]

    @pl.when(stay)
    def _():
        await_bytes(pool.at[pl.ds(0, parts)], s_cand)

    @pl.when(away)
    def _():
        await_bytes(pool.at[pl.ds(0, 2 * parts)], s_cand)
        await_bytes(anchor.at[:, inner], s_pert)

    await_bytes(out_up, s_give)
    await_bytes(rims, s_edge)

    @pl.when(up_ok)
    def _():
        await_bytes(out_up, s_up)

    @pl.when(dn_ok)
    def _():
        await_bytes(out_dn, s_dn)

    lanes = lax.broadcasted_iota(jnp.int32, (n, 128), 1)
    ranks = lax.broadcasted_iota(jnp.int32, (n, 128), 0)

    @pl.when(mine < slots)
    def _():
        await_bytes(cols_ref.at[pl.ds(0, n - 1)], r_vec)
        gram = jnp.zeros((n, 128), F32)
        for i in range(n):
            total = jnp.sum(cols_ref[...] * cols_ref[slot(i)][None], axis=(1, 2))
            if total.shape[-1] != 128:
                total = total.reshape(n, size_l, 128).sum(axis=1)
            gram = gram + jnp.where(lanes == i, jnp.sum(total, axis=1, keepdims=True), 0.0)
        mine_s[...] = gram

    @pl.when(mine >= slots)
    def _():
        mine_s[...] = jnp.zeros((n, 128), F32)

    if packed:
        row = jnp.sum(pltpu.roll(mine_s[...], 0, 1, stride=n, stride_axis=0), axis=0, keepdims=True)
        mine_v[...] = row
        rank = me * ns + tile
        reach = [(2 * m + c, ds) for m in far_first(lines) for c in range(2) for ds in range(ns) if m or c or ds]
        for dv, ds in reach:
            where = {"vec": paired(me, dv, n), "space": paired(tile, ds, ns)}
            remote(mine_v, gvec.at[rank], s_gv, r_gv, where).start()
        gvec[rank] = row
        await_bytes(gvec.at[pl.ds(0, n * ns - 1)], r_gv)
        row = gvec[0]
        for i in range(1, n * ns):
            row = row + gvec[i]
        gram = pltpu.roll(jnp.broadcast_to(row, (n, 128)), 128 - n * (n - 1), 1, stride=n, stride_axis=0)
    else:
        for d in range(1, ns):
            to = lax.rem(tile + d, ns)
            remote(mine_s, gspace.at[tile], s_gs, r_gs, {"space": to}).start()
        gspace[tile] = mine_s[...]
        await_bytes(gspace.at[pl.ds(0, ns - 1)], r_gs)
        gram = gspace[0]
        for i in range(1, ns):
            gram = gram + gspace[i]
        mine_v[...] = gram
        for d in range(1, n):
            to = lax.rem(me + d, n)
            remote(mine_v, gvec.at[me], s_gv, r_gv, {"vec": to}).start()
        gvec[me] = gram
        await_bytes(gvec.at[pl.ds(0, n - 1)], r_gv)
        gram = gvec[0]
        for i in range(1, n):
            gram = gram + gvec[i]

    a = jnp.where(lanes < n, gram / entries, 0.0) + jnp.where(lanes == ranks + n, 1.0, 0.0)
    diagonal = jnp.ones((n, 1), F32)
    for k in range(n):
        column = a[:, k : k + 1]
        diagonal = jnp.where(ranks[:, :1] == k, column, diagonal)
        factor = jnp.where(ranks[:, :1] > k, column / column[k : k + 1, :], 0.0)
        a = a - factor * a[k : k + 1, :]
    a = a / jnp.sqrt(diagonal)
    upper_ref[...] = jnp.where(lanes >= ranks, a, 0.0)[:, :n]

    @pl.when(mine < slots)
    def _():
        for i in range(n):
            total = a[i : i + 1, n : n + 1][None] * cols_ref[slot(0)]
            for j in range(1, i + 1):
                total = total + a[i : i + 1, n + j : n + j + 1][None] * cols_ref[slot(j)]
            result[i] = total

        for d in order:
            i = paired(vector, d, n)

            @pl.when((me != i) | away)
            def _():
                remote(
                    result.at[i], window(out_ref, mine), s_back, r_back, {"vec": i, "space": block}
                ).start()

        @pl.when(stay)
        def _():
            window(out_ref, mine)[...] = result[me]

    def drain(several, fewer, sem):
        @pl.when(fewer)
        def _():
            await_bytes(result.at[pl.ds(0, several - 1)], sem)

        @pl.when(jnp.logical_not(fewer))
        def _():
            await_bytes(result.at[pl.ds(0, several)], sem)

    drain(slots, stay & (mine < slots), r_back)
    drain(slots, mine < slots, s_vec)

    @pl.when(mine < slots)
    def _():
        drain(n, stay, s_back)

    if packed:
        await_bytes(gvec.at[pl.ds(0, n * ns - 1)], s_gv)
    else:
        await_bytes(gspace.at[pl.ds(0, ns - 1)], s_gs)
        await_bytes(gvec.at[pl.ds(0, n - 1)], s_gv)


def body(n, ns, perturbation, trajectory, step_order):
    pert, traj = perturbation[0], trajectory[0]
    fields, rows, cols = pert.shape
    sections = traj.shape[0]
    parts, bf = sections * (rows // HALO), traj.dtype
    chunks, layer = STEPS * parts, fields // 2
    packed = n * n <= 128 and n % 8 == 0 and n * ns <= 64
    size_f, size_l = slice_shape(n, fields, cols)
    vmem = pl.BlockSpec(memory_space=pltpu.VMEM)
    hbm = pl.BlockSpec(memory_space=pl.ANY)
    piece = pltpu.VMEM((chunks, layer, HALO, cols), bf)
    full = pltpu.VMEM((fields, rows + 2 * HALO, cols), F32)
    slices = pltpu.VMEM((n, size_f, rows, 128 * size_l), F32)
    small = pltpu.VMEM((n, 128), F32)
    dma, one = pltpu.SemaphoreType.DMA, pltpu.SemaphoreType.DMA(())
    out, upper = pl.pallas_call(
        functools.partial(whole_kernel, n, ns, float(fields * rows * cols * ns)),
        out_shape=(pltpu.VMEM(pert.shape, F32), pltpu.VMEM((n, n), F32)),
        in_specs=[hbm, hbm, hbm],
        out_specs=(vmem, vmem),
        scratch_shapes=[
            pltpu.SMEM(step_order.shape, jnp.int32),
            pltpu.VMEM((STEPS * sections, fields, rows + 2 * HALO, cols), bf),
            pltpu.VMEM((2, parts, layer, HALO, cols), bf),
            piece, piece, piece, piece, piece,
            pltpu.VMEM((fields // 2, rows + 4 * HALO, cols), bf),
            pltpu.VMEM((STEPS * sections, fields, 2 * HALO, cols), bf),
            full, pltpu.VMEM((2, *full.shape), F32),
            pltpu.VMEM(pert.shape, F32), slices, slices,
            pltpu.VMEM((ns, n, 128), F32),
            pltpu.VMEM((n * ns, 1, 128) if packed else (n, n, 128), F32),
            small,
            pltpu.VMEM((1, 128), F32) if packed else small,
            one, dma((parts,)), dma((chunks,)), dma((chunks,)), dma((STEPS * sections,)),
            one, one, one, one, one, one,
            one, one, one, one, one, one, one, one, one, one, one,
        ],
        compiler_params=pltpu.CompilerParams(collective_id=0, has_side_effects=True),
        name="whole",
    )(step_order, traj, pert)

    def finish(back_ref, upper_ref, out_ref, factor_ref, sems):
        copies = [
            pltpu.make_async_copy(back_ref, out_ref, sems.at[0]),
            pltpu.make_async_copy(upper_ref, factor_ref, sems.at[1]),
        ]
        for copy in copies:
            copy.start()
        for copy in copies:
            copy.wait()

    out, factor = pl.pallas_call(
        finish,
        out_shape=(jax.ShapeDtypeStruct(pert.shape, F32), jax.ShapeDtypeStruct((n, n), F32)),
        in_specs=[vmem, vmem],
        out_specs=(hbm, hbm),
        scratch_shapes=[dma((2,))],
        name="finish",
    )(
        pltpu.with_memory_space_constraint(out, pltpu.VMEM),
        pltpu.with_memory_space_constraint(upper, pltpu.VMEM),
    )
    return out[None], factor


def solution(mesh):
    n, ns = mesh.shape["vec"], mesh.shape["space"]
    in_specs = (P("vec", None, "space", None), P("vec", None, None, "space", None), P())
    out_specs = (P("vec", None, "space", None), P())
    return jax.shard_map(
        functools.partial(body, n, ns), mesh=mesh, in_specs=in_specs, out_specs=out_specs, check_vma=False
    )
```

```python
import functools

import jax
import jax.numpy as jnp
from jax import lax
from jax.experimental import pallas as pl
from jax.experimental.pallas import tpu as pltpu
from jax.sharding import PartitionSpec as P

STEPS = 2
SECTIONS = 3
LAG_UP = 6
LAG_DN = 6
RUN_LAG_END = 8
RUN_LAG_MID = 17
HALO = 8

GRAVITY_TOP = 1.0
GRAVITY_LOW = 0.5
DEPTH_TOP = 1.0
DEPTH_LOW = 1.0
CORIOLIS = 0.3
TIME_STEP = 0.25

MESH = pl.DeviceIdType.MESH
F32 = jnp.float32


def remote(src, dst, send, recv, target):
    return pltpu.make_async_remote_copy(
        src_ref=src, dst_ref=dst, send_sem=send, recv_sem=recv, device_id=target, device_id_type=MESH
    )


def await_bytes(ref, sem):
    pltpu.make_async_copy(ref, ref, sem).wait()


def twice_dx(field):
    count = field.shape[0]
    return pltpu.roll(field, count - 1, 0) - pltpu.roll(field, 1, 0)


def twice_dy(field):
    count = field.shape[1]
    return pltpu.roll(field, count - 1, 1) - pltpu.roll(field, 1, 1)


def tangent(layer, base, state, top, low):
    pressure = GRAVITY_TOP * (top + low)
    if layer:
        pressure = pressure + GRAVITY_LOW * low
    depth = base[0] + (DEPTH_TOP, DEPTH_LOW)[layer]
    u, v = base[1], base[2]
    dh, du, dv = state
    return [
        twice_dx(depth * du + dh * u) + twice_dy(depth * dv + dh * v),
        (u * twice_dx(du) + du * twice_dx(u)) + (v * twice_dy(du) + dv * twice_dy(u))
        + twice_dx(pressure) - (2 * CORIOLIS) * dv,
        (u * twice_dx(dv) + du * twice_dx(v)) + (v * twice_dy(dv) + dv * twice_dy(v))
        + twice_dy(pressure) + (2 * CORIOLIS) * du,
    ]


def slice_shape(n, fields, cols):
    lanes = cols // 128
    best = None
    for f in range(1, fields + 1):
        for l in range(1, lanes + 1):
            if fields % f or lanes % l or (fields // f) * (lanes // l) > n:
                continue
            if best is None or f * l < best[0] * best[1]:
                best = (f, l)
    return best


def paired(value, mask, count):
    if count & (count - 1):
        return lax.rem(value + mask, count)
    made, bit = 0, 1
    while bit < count:
        digit = lax.rem(lax.div(value, bit), 2)
        made = made + bit * (1 - digit if mask & bit else digit)
        bit *= 2
    return made


def far_first(count):
    return sorted(range(count), key=lambda m: (-m.bit_length(), m))


def whole_kernel(
    n, ns, entries, order_in, traj_ref, pert_ref,
    out_ref, upper_ref,
    order_ref, main, cand, in_up, in_dn, out_up, out_dn, pool, fresh, rims, anchor, work,
    x_ref, cols_ref, result, gspace, gvec, mine_s, mine_v,
    r_order, r_cand, r_up, r_dn, r_sec, r_pert, r_side, r_vec, r_gs, r_gv, r_back,
    s_cand, s_pert, s_side, s_up, s_dn, s_give, s_edge, s_vec, s_gs, s_gv, s_back,
):
    me = lax.axis_index("vec")
    tile = lax.axis_index("space")
    fields, rows, cols = pert_ref.shape
    half = fields // 2
    per = rows // HALO
    parts = SECTIONS * per
    chunks = STEPS * parts
    lines, places = n // 2, ns // 2
    side, line = lax.rem(me, 2), me // 2
    core, place = lax.rem(tile, 2), tile // 2
    flip = lax.rem(place, 2)

    def differs(a, b):
        return a + b - 2 * a * b

    home = differs(side, flip)
    stay = core == home
    away = core != home
    block = 2 * place + home
    vector = 2 * line + differs(core, flip)
    sibling = {"space": 2 * place + 1 - core}
    up_ok = line < lines - 1
    dn_ok = line > 0

    def worker(v, t):
        p = t // 2
        turn = lax.rem(p, 2)
        return {
            "vec": 2 * (v // 2) + differs(lax.rem(t, 2), turn),
            "space": 2 * p + differs(lax.rem(v, 2), turn),
        }

    barrier = pltpu.get_barrier_semaphore()
    near = sorted({0, 1 % places, places - 1})
    count = 0
    for across in range(2):
        for step in near:
            for c in range(2):
                if (across == 0 and step == 0 and c == 0) or (across and step):
                    continue
                where = {
                    "vec": me + across * (1 - 2 * side),
                    "space": 2 * lax.rem(place + step, places) + lax.rem(core + c, 2),
                }
                pl.semaphore_signal(barrier, inc=1, device_id=where, device_id_type=MESH)
                count += 1

    @pl.when(up_ok)
    def _():
        pl.semaphore_signal(barrier, inc=1, device_id={"vec": me + 2}, device_id_type=MESH)

    @pl.when(dn_ok)
    def _():
        pl.semaphore_signal(barrier, inc=1, device_id={"vec": me - 2}, device_id_type=MESH)

    inner = pl.ds(HALO, rows)

    def band(w):
        return pl.multiple_of(HALO * jnp.where(w == 0, 0, jnp.where(w == 1, per - 1, w - 1)), HALO)

    def origin(p, layer):
        return traj_ref.at[lax.div(p, per), pl.ds(half * layer, half), pl.ds(band(lax.rem(p, per)), HALO)]

    order_copy = pltpu.make_async_copy(order_in, order_ref, r_order)
    order_copy.start()

    @pl.when(stay)
    def _():
        @pl.loop(0, parts)
        def _(p):
            pltpu.make_async_copy(origin(p, core), cand.at[0, p], r_cand.at[p]).start()

        pltpu.make_async_copy(pert_ref, anchor.at[:, inner], r_pert).start()

    pl.semaphore_wait(barrier, count + up_ok.astype(jnp.int32) + dn_ok.astype(jnp.int32))

    other = me + 1 - 2 * side

    @pl.when(stay)
    def _():
        @pl.loop(0, parts)
        def _(p):
            remote(
                origin(p, 1 - core), cand.at[0, p], s_cand, r_cand.at[p], sibling
            ).start()

    @pl.when(away)
    def _():
        @pl.loop(0, parts)
        def _(p):
            for c in range(2):
                remote(
                    origin(p, c), cand.at[1, p], s_cand, r_cand.at[p],
                    {"vec": other, "space": 2 * place + c},
                ).start()

    @pl.when(away)
    def _():
        remote(
            pert_ref, anchor.at[:, inner], s_pert, r_pert,
            {"vec": other, "space": 2 * place + 1 - core},
        ).start()

    def go_up(c):
        return remote(out_up.at[c], in_up.at[c], s_up, r_up.at[c], {"vec": me + 2})

    def go_dn(c):
        return remote(out_dn.at[c], in_dn.at[c], s_dn, r_dn.at[c], {"vec": me - 2})

    def owner_of(c):
        return jnp.where(c >= parts, order_ref[1], order_ref[0])

    def candidate(c):
        p = lax.rem(c, parts)
        return jnp.where(owner_of(c) == me, cand[0, p], cand[1, p])

    def inside(c):
        return (c >= 0) & (c < chunks)

    first_block = worker(vector, lax.rem(block + 1, ns))
    last_block = worker(vector, lax.rem(block + ns - 1, ns))
    own_layer = pl.ds(half * core, half)

    run_lag = jnp.where(up_ok & dn_ok, RUN_LAG_MID, RUN_LAG_END)
    up_lag = LAG_UP * line
    dn_lag = LAG_DN * (lines - 1 - line)
    near_lag = jnp.where(up_ok & dn_ok, jnp.minimum(up_lag, dn_lag), 0)
    far_lag = jnp.maximum(up_lag, dn_lag)
    most = max(
        max(LAG_UP * l, LAG_DN * (lines - 1 - l)) + (RUN_LAG_MID if 0 < l < lines - 1 else RUN_LAG_END)
        for l in range(lines)
    )

    def rates(number, layer):
        now = lax.rem(number, 2)
        at = half * layer
        base = [main[number, at + f].astype(F32) for f in range(half)]
        state = [work[now, at + f] for f in range(half)]
        top = state[0] if layer == 0 else work[now, 0]
        low = state[0] if layer == 1 else work[now, half]
        return state, tangent(layer, base, state, top, low)

    def advance(number, layer):
        section = lax.rem(number, SECTIONS)
        state, change = rates(number, layer)
        keep = jnp.where(section == 0, 0.0, jnp.where(section == 1, 0.75, 1.0 / 3.0)).astype(F32)
        take = jnp.where(section == 0, 1.0, jnp.where(section == 1, 0.25, 2.0 / 3.0)).astype(F32)
        for f in range(half):
            at = half * layer + f
            work[1 - lax.rem(number, 2), at] = keep * anchor[at] + take * (state[f] - (0.5 * TIME_STEP) * change[f])

        @pl.when(section == SECTIONS - 1)
        def _():
            for f in range(half):
                at = half * layer + f
                anchor[at] = work[1 - lax.rem(number, 2), at]

    order_copy.wait()

    @pl.loop(0, most + chunks - per + 1)
    def _(t):
        c_pair = t - near_lag
        c_up = t - up_lag
        c_dn = t - dn_lag
        c_fin = t - far_lag
        c_run = c_fin - run_lag

        @pl.when((c_pair >= 0) & (c_pair < parts))
        def _():
            await_bytes(cand.at[:, c_pair], r_cand.at[c_pair])

        @pl.when(inside(c_up))
        def _():
            @pl.when(dn_ok)
            def _():
                go_up(c_up).wait_recv()

            @pl.when(up_ok)
            def _():
                here = lax.div(owner_of(c_up), 2) == line
                out_up[c_up] = jnp.where(here, candidate(c_up), in_up[c_up])
                go_up(c_up).start()

        @pl.when(inside(c_dn))
        def _():
            @pl.when(up_ok)
            def _():
                go_dn(c_dn).wait_recv()

            @pl.when(dn_ok)
            def _():
                here = lax.div(owner_of(c_dn), 2) == line
                out_dn[c_dn] = jnp.where(here, candidate(c_dn), in_dn[c_dn])
                go_dn(c_dn).start()

        @pl.when(inside(c_fin))
        def _():
            at = lax.div(owner_of(c_fin), 2)
            q, w = lax.div(c_fin, per), lax.rem(c_fin, per)
            spot = main.at[q, own_layer, pl.ds(HALO + band(w), HALO)]
            spot[...] = jnp.where(
                at == line, candidate(c_fin), jnp.where(at < line, in_up[c_fin], in_dn[c_fin])
            )
            remote(spot, spot, s_give, r_sec.at[q], sibling).start()

            for turn, target, src, dst in ((0, last_block, HALO, HALO + rows), (1, first_block, rows, 0)):

                @pl.when(w == turn)
                def _():
                    for c in range(2):
                        remote(
                            main.at[q, own_layer, pl.ds(src, HALO)],
                            main.at[q, own_layer, pl.ds(dst, HALO)],
                            s_edge, r_sec.at[q],
                            {"vec": target["vec"], "space": 2 * (target["space"] // 2) + c},
                        ).start()

        @pl.when(c_fin == per - 1)
        def _():
            await_bytes(anchor.at[:, inner], r_pert)
            for target, src, dst in ((first_block, rows, 0), (last_block, HALO, HALO + rows)):
                remote(
                    anchor.at[:, pl.ds(src, HALO)], anchor.at[:, pl.ds(dst, HALO)], s_side, r_side, target
                ).start()

        @pl.when(c_run == per - 1)
        def _():
            await_bytes(anchor.at[:, pl.ds(0, 2 * HALO)], r_side)
            await_bytes(anchor.at[:, pl.ds(0, 2 * HALO)], s_side)
            work[0] = anchor[...]

        @pl.when((c_run >= per - 1) & (c_run < chunks - 1) & (lax.rem(c_run, per) == per - 1))
        def _():
            number = lax.div(c_run, per)
            await_bytes(fresh, r_sec.at[number])
            advance(number, 0)

        @pl.when((c_run >= per) & (c_run < chunks) & (lax.rem(c_run, per) == 0))
        def _():
            advance(lax.div(c_run, per) - 1, 1)

    size_f, size_l = slice_shape(n, fields, cols)
    across = cols // (128 * size_l)
    slots = (fields // size_f) * across

    def share(v):
        return lines * lax.rem(v, 2) + lax.div(v, 2)

    mine = share(2 * line + core)
    packed = n * n <= 128 and n % 8 == 0 and n * ns <= 64

    def slot(v):
        return n - 1 - v if packed else v

    def window(ref, j):
        f = pl.multiple_of(lax.div(j, across) * size_f, size_f)
        l = pl.multiple_of(lax.rem(j, across) * (128 * size_l), 128 * size_l)
        return ref.at[pl.ds(f, size_f), :, pl.ds(l, 128 * size_l)]

    def spread(d):
        to = paired(2 * line + core, d, n)
        return share(to), {"vec": 2 * (to // 2) + side, "space": 2 * place + lax.rem(to, 2)}

    order = [2 * m + c for m in far_first(lines) for c in range(2)]
    final = STEPS * SECTIONS - 1
    await_bytes(fresh, r_sec.at[final])
    mid = slice(HALO, HALO + rows)
    for layer in range(2):
        state, change = rates(final, layer)
        for f in range(half):
            at = half * layer + f
            x_ref[at] = anchor[at, mid] * (1.0 / 3.0) + (2.0 / 3.0) * (state[f][mid] - (0.5 * TIME_STEP) * change[f][mid])
        if half % size_f and layer == 0:
            continue
        for d in order:
            to, where = spread(d)
            mine_now = (to < slots) & (to // across * size_f // half == layer) if half % size_f == 0 else to < slots
            if d:

                @pl.when(mine_now)
                def _():
                    remote(window(x_ref, to), cols_ref.at[slot(vector)], s_vec, r_vec, where).start()

    @pl.when(mine < slots)
    def _():
        cols_ref[slot(vector)] = window(x_ref, mine)[...]

    @pl.when(stay)
    def _():
        await_bytes(pool.at[pl.ds(0, parts)], s_cand)

    @pl.when(away)
    def _():
        await_bytes(pool.at[pl.ds(0, 2 * parts)], s_cand)
        await_bytes(anchor.at[:, inner], s_pert)

    await_bytes(out_up, s_give)
    await_bytes(rims, s_edge)

    @pl.when(up_ok)
    def _():
        await_bytes(out_up, s_up)

    @pl.when(dn_ok)
    def _():
        await_bytes(out_dn, s_dn)

    lanes = lax.broadcasted_iota(jnp.int32, (n, 128), 1)
    ranks = lax.broadcasted_iota(jnp.int32, (n, 128), 0)

    @pl.when(mine < slots)
    def _():
        await_bytes(cols_ref.at[pl.ds(0, n - 1)], r_vec)
        gram = jnp.zeros((n, 128), F32)
        for i in range(n):
            total = jnp.sum(cols_ref[...] * cols_ref[slot(i)][None], axis=(1, 2))
            if total.shape[-1] != 128:
                total = total.reshape(n, size_l, 128).sum(axis=1)
            gram = gram + jnp.where(lanes == i, jnp.sum(total, axis=1, keepdims=True), 0.0)
        mine_s[...] = gram

    @pl.when(mine >= slots)
    def _():
        mine_s[...] = jnp.zeros((n, 128), F32)

    if packed:
        row = jnp.sum(pltpu.roll(mine_s[...], 0, 1, stride=n, stride_axis=0), axis=0, keepdims=True)
        mine_v[...] = row
        rank = me * ns + tile
        reach = [(2 * m + c, ds) for m in far_first(lines) for c in range(2) for ds in range(ns) if m or c or ds]
        for dv, ds in reach:
            where = {"vec": paired(me, dv, n), "space": paired(tile, ds, ns)}
            remote(mine_v, gvec.at[rank], s_gv, r_gv, where).start()
        gvec[rank] = row
        await_bytes(gvec.at[pl.ds(0, n * ns - 1)], r_gv)
        rows_in = [gvec[i] for i in range(n * ns)]
        while len(rows_in) > 1:
            pairs = [a + b for a, b in zip(rows_in[::2], rows_in[1::2])]
            rows_in = pairs + rows_in[len(pairs) * 2 :]
        row = rows_in[0]
        gram = pltpu.roll(jnp.broadcast_to(row, (n, 128)), 128 - n * (n - 1), 1, stride=n, stride_axis=0)
    else:
        for d in range(1, ns):
            to = lax.rem(tile + d, ns)
            remote(mine_s, gspace.at[tile], s_gs, r_gs, {"space": to}).start()
        gspace[tile] = mine_s[...]
        await_bytes(gspace.at[pl.ds(0, ns - 1)], r_gs)
        gram = gspace[0]
        for i in range(1, ns):
            gram = gram + gspace[i]
        mine_v[...] = gram
        for d in range(1, n):
            to = lax.rem(me + d, n)
            remote(mine_v, gvec.at[me], s_gv, r_gv, {"vec": to}).start()
        gvec[me] = gram
        await_bytes(gvec.at[pl.ds(0, n - 1)], r_gv)
        gram = gvec[0]
        for i in range(1, n):
            gram = gram + gvec[i]

    a = jnp.where(lanes < n, gram / entries, 0.0) + jnp.where(lanes == ranks + n, 1.0, 0.0)
    diagonal = jnp.ones((n, 1), F32)
    for k in range(n):
        column = a[:, k : k + 1]
        diagonal = jnp.where(ranks[:, :1] == k, column, diagonal)
        factor = jnp.where(ranks[:, :1] > k, column / column[k : k + 1, :], 0.0)
        a = a - factor * a[k : k + 1, :]
    a = a / jnp.sqrt(diagonal)
    upper_ref[...] = jnp.where(lanes >= ranks, a, 0.0)[:, :n]

    @pl.when(mine < slots)
    def _():
        for i in range(n):
            total = a[i : i + 1, n : n + 1][None] * cols_ref[slot(0)]
            for j in range(1, i + 1):
                total = total + a[i : i + 1, n + j : n + j + 1][None] * cols_ref[slot(j)]
            result[i] = total

        for d in order:
            i = paired(vector, d, n)

            @pl.when((me != i) | away)
            def _():
                remote(
                    result.at[i], window(out_ref, mine), s_back, r_back, {"vec": i, "space": block}
                ).start()

        @pl.when(stay)
        def _():
            window(out_ref, mine)[...] = result[me]

    def drain(several, fewer, sem):
        @pl.when(fewer)
        def _():
            await_bytes(result.at[pl.ds(0, several - 1)], sem)

        @pl.when(jnp.logical_not(fewer))
        def _():
            await_bytes(result.at[pl.ds(0, several)], sem)

    drain(slots, stay & (mine < slots), r_back)
    drain(slots, mine < slots, s_vec)

    @pl.when(mine < slots)
    def _():
        drain(n, stay, s_back)

    if packed:
        await_bytes(gvec.at[pl.ds(0, n * ns - 1)], s_gv)
    else:
        await_bytes(gspace.at[pl.ds(0, ns - 1)], s_gs)
        await_bytes(gvec.at[pl.ds(0, n - 1)], s_gv)


def body(n, ns, perturbation, trajectory, step_order):
    pert, traj = perturbation[0], trajectory[0]
    fields, rows, cols = pert.shape
    sections = traj.shape[0]
    parts, bf = sections * (rows // HALO), traj.dtype
    chunks, layer = STEPS * parts, fields // 2
    packed = n * n <= 128 and n % 8 == 0 and n * ns <= 64
    size_f, size_l = slice_shape(n, fields, cols)
    vmem = pl.BlockSpec(memory_space=pltpu.VMEM)
    hbm = pl.BlockSpec(memory_space=pl.ANY)
    piece = pltpu.VMEM((chunks, layer, HALO, cols), bf)
    full = pltpu.VMEM((fields, rows + 2 * HALO, cols), F32)
    slices = pltpu.VMEM((n, size_f, rows, 128 * size_l), F32)
    small = pltpu.VMEM((n, 128), F32)
    dma, one = pltpu.SemaphoreType.DMA, pltpu.SemaphoreType.DMA(())
    out, upper = pl.pallas_call(
        functools.partial(whole_kernel, n, ns, float(fields * rows * cols * ns)),
        out_shape=(pltpu.VMEM(pert.shape, F32), pltpu.VMEM((n, n), F32)),
        in_specs=[hbm, hbm, hbm],
        out_specs=(vmem, vmem),
        scratch_shapes=[
            pltpu.SMEM(step_order.shape, jnp.int32),
            pltpu.VMEM((STEPS * sections, fields, rows + 2 * HALO, cols), bf),
            pltpu.VMEM((2, parts, layer, HALO, cols), bf),
            piece, piece, piece, piece, piece,
            pltpu.VMEM((fields // 2, rows + 4 * HALO, cols), bf),
            pltpu.VMEM((STEPS * sections, fields, 2 * HALO, cols), bf),
            full, pltpu.VMEM((2, *full.shape), F32),
            pltpu.VMEM(pert.shape, F32), slices, slices,
            pltpu.VMEM((ns, n, 128), F32),
            pltpu.VMEM((n * ns, 1, 128) if packed else (n, n, 128), F32),
            small,
            pltpu.VMEM((1, 128), F32) if packed else small,
            one, dma((parts,)), dma((chunks,)), dma((chunks,)), dma((STEPS * sections,)),
            one, one, one, one, one, one,
            one, one, one, one, one, one, one, one, one, one, one,
        ],
        compiler_params=pltpu.CompilerParams(collective_id=0, has_side_effects=True),
        name="whole",
    )(step_order, traj, pert)

    def finish(back_ref, upper_ref, out_ref, factor_ref, sems):
        copies = [
            pltpu.make_async_copy(back_ref, out_ref, sems.at[0]),
            pltpu.make_async_copy(upper_ref, factor_ref, sems.at[1]),
        ]
        for copy in copies:
            copy.start()
        for copy in copies:
            copy.wait()

    out, factor = pl.pallas_call(
        finish,
        out_shape=(jax.ShapeDtypeStruct(pert.shape, F32), jax.ShapeDtypeStruct((n, n), F32)),
        in_specs=[vmem, vmem],
        out_specs=(hbm, hbm),
        scratch_shapes=[dma((2,))],
        name="finish",
    )(
        pltpu.with_memory_space_constraint(out, pltpu.VMEM),
        pltpu.with_memory_space_constraint(upper, pltpu.VMEM),
    )
    return out[None], factor


def solution(mesh):
    n, ns = mesh.shape["vec"], mesh.shape["space"]
    in_specs = (P("vec", None, "space", None), P("vec", None, None, "space", None), P())
    out_specs = (P("vec", None, "space", None), P())
    return jax.shard_map(
        functools.partial(body, n, ns), mesh=mesh, in_specs=in_specs, out_specs=out_specs, check_vma=False
    )
```
